32 devices in a mesh: dp: 16 (over z, y, core), ctx: 2 (over x).
Axes of the slice: x: 2, y: 2, z: 4, core: 2. Of those that a mesh axis runs over, the one named last changes fastest.
Arguments:
- tokens: bfloat16 [32, 1024, 1024], P('dp', 'ctx'), may hold values from -6 to 6
- cotangent: bfloat16 [32, 1024, 1024], P('dp', 'ctx'), may hold values from -6 to 6
- w_qkv: bfloat16 [1024, 3072], P(('dp', 'ctx')), may hold values from -0.1875 to 0.1875
- w_out: bfloat16 [1024, 1024], P(('dp', 'ctx')), may hold values from -3 to 3
- w_gate: bfloat16 [1024, 2624], P(('dp', 'ctx')), may hold values from -0.1875 to 0.1875
- w_up: bfloat16 [1024, 2624], P(('dp', 'ctx')), may hold values from -0.1875 to 0.1875
- w_down: bfloat16 [2624, 1024], P(None, ('dp', 'ctx')), may hold values from -0.125 to 0.125
- gain_one: bfloat16 [1024], P(('dp', 'ctx')), may hold values from 0.099609375 to 1.8984375
- gain_two: bfloat16 [1024], P(('dp', 'ctx')), may hold values from 0.099609375 to 1.8984375
Outputs:
- result: bfloat16 [32, 1024, 1024], P('dp', 'ctx')
- input_grad: bfloat16 [32, 1024, 1024], P('dp', 'ctx')
- grad_qkv: float32 [1024, 3072], P(('dp', 'ctx'))
- grad_out: float32 [1024, 1024], P(('dp', 'ctx'))
- grad_gate: float32 [1024, 2624], P(('dp', 'ctx'))
- grad_up: float32 [1024, 2624], P(('dp', 'ctx'))
- grad_down: float32 [2624, 1024], P(None, ('dp', 'ctx'))
- grad_gain_one: float32 [1024], P(('dp', 'ctx'))
- grad_gain_two: float32 [1024], P(('dp', 'ctx'))
The draws below stay inside these ranges and needn't reach their ends.
All inputs are finite; a program needn't handle non-finite values.
Results may differ from the reference program's by a relative error of at most 0.025.
Values may be sent and summed in bfloat16 or wider, within the bound.
No kernel may reach another device: no remote copies, remote signals or barrier semaphores. Data moves between devices by JAX's collectives and lax.ppermute only.
A program may use at most 448 MiB of HBM per device.

```python
import math
import jax
import jax.numpy as jnp
from jax import lax

D = 1024
HEADS = 16
HEAD_DIM = 64
FF = 2624
LEN = 1024
SEQS = 32


def levels(stream_key, dims, split, least, top_value):
    def one(dim, parts):
        steps = jax.random.uniform(jax.random.fold_in(jax.random.fold_in(stream_key, 6), dim), (parts,), jnp.float32, least / len(split), top_value / len(split))
        return jnp.repeat(jnp.exp(steps), dims[dim] // parts).reshape((-1,) + (1,) * (len(dims) - dim - 1))

    gain = one(*split[0])
    for cut in split[1:]:
        gain = gain * one(*cut)
    return gain


def bell_draw(own_key, dims, spread, bound, shards=(), held_as=jnp.bfloat16):
    gain = levels(own_key, dims, shards, -0.22, 0.18) if shards else 1.0
    array = jax.random.normal(own_key, dims, jnp.float32) * spread * gain
    return jnp.minimum(jnp.maximum(array, -bound), bound).astype(held_as)


def setup_inputs(seed: int = 0) -> dict:
    key_list = jax.random.split(jax.random.key(seed), 10)
    return {
        "tokens": bell_draw(key_list[0], (SEQS, LEN, D), 1.0, 6.0, ((0, 16), (1, 2))),
        "cotangent": bell_draw(key_list[1], (SEQS, LEN, D), 1.0, 6.0, ((0, 16), (1, 2))),
        "w_qkv": bell_draw(key_list[2], (D, 3 * D), D ** -0.5, 0.1875, ((0, 32),)),
        "w_out": bell_draw(key_list[3], (D, D), 4 ** -0.5, 3.0, ((0, 32),)),
        "w_gate": bell_draw(key_list[4], (D, FF), D ** -0.5, 0.1875, ((0, 32),)),
        "w_up": bell_draw(key_list[5], (D, FF), D ** -0.5, 0.1875, ((0, 32),)),
        "w_down": bell_draw(key_list[6], (FF, D), FF ** -0.5, 0.125, ((1, 32),)),
        "gain_one": jnp.clip(1.0 + 0.18 * jax.random.normal(key_list[7], (D,), jnp.float32), 0.099609375, 1.8984375).astype(jnp.bfloat16),
        "gain_two": jnp.clip(1.0 + 0.18 * jax.random.normal(key_list[8], (D,), jnp.float32), 0.099609375, 1.8984375).astype(jnp.bfloat16),
    }


THETA = 160000.0
EPSILON = 1e-05
HIGHEST = lax.Precision.HIGHEST

@jax.custom_vjp
def low(v):
    return lax.optimization_barrier(v.astype(jnp.bfloat16)).astype(jnp.float32)

@jax.custom_vjp
def low_back(v):
    return v

def low_keep(v):
    return (low(v), None)

def low_pass(kept, grad):
    return (grad,)

def back_keep(v):
    return (v, None)

def back_low(kept, grad):
    return (low(grad),)
low.defvjp(low_keep, low_pass)
low_back.defvjp(back_keep, back_low)

def product(left, right):
    return jnp.dot(left, right, precision=HIGHEST)

def rotary_tables(length, offset, head_size):
    halfway = head_size // 2
    frequency = jnp.exp(jnp.arange(halfway).astype(jnp.float32) * (-2.0 * math.log(THETA) / head_size))
    position = (offset + jnp.arange(length)).astype(jnp.float32)
    angles = position[:, None] * frequency[None, :]
    cosine = jnp.cos(angles)
    sine_table = jnp.sin(angles)
    return (jnp.concatenate([cosine, cosine], -1), jnp.concatenate([sine_table, sine_table], -1))

def rotate_half(values):
    halfway = values.shape[-1] // 2
    return jnp.concatenate([-values[..., halfway:], values[..., :halfway]], -1)

def turn(values, cosine, sine_table):
    return values * cosine[:, None, :] + rotate_half(values) * sine_table[:, None, :]

def standardize(values):
    centered = values - lax.optimization_barrier(jnp.mean(values, -1, keepdims=True))
    inverse = lax.rsqrt(lax.optimization_barrier(jnp.mean(centered * centered, -1, keepdims=True)) + EPSILON)
    return (centered * inverse, inverse)

def attend(triple):
    queries, key_block, value_block = triple
    scores = low_back(jnp.einsum('qhd,khd->hqk', queries, key_block, precision=HIGHEST) * 0.125)
    weights = low(jax.nn.softmax(scores, -1))
    return jnp.einsum('hqk,khd->qhd', weights, value_block, precision=HIGHEST)

def block(params, group):
    w_qkv, w_out, w_gate, w_up, w_down, gain_one, gain_two = params
    count, length, width = group.shape
    flat_rows = group.reshape(count * length, width)
    normed_one, _ = standardize(flat_rows)
    first = low(normed_one * gain_one)
    merged = low_back(product(first, w_qkv))
    cosine, sine_table = rotary_tables(length, 0, HEAD_DIM)

    def section(part_no):
        return merged[:, part_no * width:(part_no + 1) * width].reshape(count, length, HEADS, HEAD_DIM)
    queries = low(turn(section(0), cosine, sine_table))
    key_part = low(turn(section(1), cosine, sine_table))
    value_part = low(section(2))
    mixed = lax.map(jax.checkpoint(attend), (queries, key_part, value_part))
    attended = low(low_back(mixed.reshape(count * length, width)))
    residual = flat_rows + low_back(product(attended, w_out))
    normed_two, _ = standardize(residual)
    second = low(normed_two * gain_two)
    gate_val = low_back(product(second, w_gate))
    up_val = low_back(product(second, w_up))
    hidden = low(jax.nn.gelu(gate_val, approximate=False) * up_val)
    outcome = residual + low_back(product(hidden, w_down))
    return outcome.reshape(count, length, width)

def reference(tokens, cotangent, w_qkv, w_out, w_gate, w_up, w_down, gain_one, gain_two):
    params = tuple((weight.astype(jnp.float32) for weight in (w_qkv, w_out, w_gate, w_up, w_down, gain_one, gain_two)))
    groups = SEQS // 4
    inputs = tokens.astype(jnp.float32).reshape(groups, 4, LEN, D)

    def forward(weights_in, data_in):
        return lax.map(jax.checkpoint(lambda group: block(weights_in, group)), data_in)
    outcome, pullback = jax.vjp(forward, params, inputs)
    weight_grads, input_grads = pullback(cotangent.astype(jnp.float32).reshape(groups, 4, LEN, D))
    return (outcome.reshape(SEQS, LEN, D).astype(jnp.bfloat16), input_grads.reshape(SEQS, LEN, D).astype(jnp.bfloat16), weight_grads[0], weight_grads[1], weight_grads[2], weight_grads[3], weight_grads[4], weight_grads[5], weight_grads[6])
```

```python
import functools
import math

import jax
import jax.numpy as jnp
from jax import lax
from jax.experimental import pallas as pl
from jax.experimental.pallas import tpu as pltpu
from jax.sharding import PartitionSpec as P

HEADS = 16
HEAD_DIM = 64


THETA = 160000.0
EPSILON = 1e-05


def rotary_tables(length, offset, head_size):
    halfway = head_size // 2
    frequency = jnp.exp(
        jnp.arange(halfway).astype(jnp.float32) * (-2.0 * math.log(THETA) / head_size)
    )
    position = (offset + jnp.arange(length)).astype(jnp.float32)
    angles = position[:, None] * frequency[None, :]
    cosine = jnp.cos(angles)
    sine_table = jnp.sin(angles)
    return (jnp.concatenate([cosine, cosine], -1), jnp.concatenate([sine_table, sine_table], -1))


def rotate_half(values):
    halfway = values.shape[-1] // 2
    return jnp.concatenate([-values[..., halfway:], values[..., :halfway]], -1)


def turn(values, cosine, sine_table):
    return values * cosine[:, None, :] + rotate_half(values) * sine_table[:, None, :]


def unturn(values, cosine, sine_table):
    return values * cosine[:, None, :] - rotate_half(values) * sine_table[:, None, :]


def standardize(values):
    centered = values - jnp.mean(values, -1, keepdims=True)
    inverse = lax.rsqrt(jnp.mean(centered * centered, -1, keepdims=True) + EPSILON)
    return (centered * inverse, inverse)


def norm_back(grad_normed, normed, inverse, gain_full):
    scaled = grad_normed * gain_full
    inner = (
        scaled
        - jnp.mean(scaled, -1, keepdims=True)
        - normed * jnp.mean(scaled * normed, -1, keepdims=True)
    )
    return (inverse * inner, jnp.sum(grad_normed * normed, 0))


def against(left, weight):
    return lax.dot_general(
        left, weight, (((1,), (1,)), ((), ())), preferred_element_type=jnp.float32
    )


def outer_sum(left, right):
    return lax.dot_general(
        left, right, (((0,), (0,)), ((), ())), preferred_element_type=jnp.float32
    )


def body(tokens, cotangent, w_qkv, w_out, w_gate, w_up, w_down, gain_one, gain_two):
    members, local_len, width = tokens.shape
    rows = members * local_len
    shards = (w_qkv, w_out, w_gate, w_up, w_down, gain_one, gain_two)
    offset = lax.axis_index("ctx") * local_len
    cosine, sine_table = rotary_tables(local_len, offset, HEAD_DIM)
    current = (
        lax.all_gather(shards[0], ("dp", "ctx"), axis=0, tiled=True),
        lax.all_gather(shards[1], ("dp", "ctx"), axis=0, tiled=True),
        lax.all_gather(shards[2], ("dp", "ctx"), axis=0, tiled=True),
        lax.all_gather(shards[3], ("dp", "ctx"), axis=0, tiled=True),
        lax.all_gather(shards[4], ("dp", "ctx"), axis=1, tiled=True),
        lax.all_gather(shards[5], ("dp", "ctx"), axis=0, tiled=True),
        lax.all_gather(shards[6], ("dp", "ctx"), axis=0, tiled=True),
    )
    full_qkv, full_out, full_gate, full_up, full_down, full_one, full_two = current
    inputs_f = tokens.astype(jnp.float32).reshape(rows, width)
    normed_one, inverse_one = standardize(inputs_f)
    first = (normed_one * full_one.astype(jnp.float32)).astype(jnp.bfloat16)
    merged = jnp.dot(first, full_qkv, preferred_element_type=jnp.float32)
    queries = turn(
        merged[:, :width].reshape(members, local_len, HEADS, HEAD_DIM), cosine, sine_table
    ).astype(jnp.bfloat16)
    key_own = turn(
        merged[:, width : 2 * width].reshape(members, local_len, HEADS, HEAD_DIM),
        cosine,
        sine_table,
    ).astype(jnp.bfloat16)
    value_own = (
        merged[:, 2 * width :].astype(jnp.bfloat16).reshape(members, local_len, HEADS, HEAD_DIM)
    )
    key_all, value_all = (
        lax.all_gather(key_own.reshape(members, local_len, width), "ctx", axis=1, tiled=True),
        lax.all_gather(value_own.reshape(members, local_len, width), "ctx", axis=1, tiled=True),
    )
    full_len = key_all.shape[1]
    key_heads = key_all.reshape(members, full_len, HEADS, HEAD_DIM)
    value_heads = value_all.reshape(members, full_len, HEADS, HEAD_DIM)
    scores = (
        jnp.einsum("bqhd,bkhd->bhqk", queries, key_heads, preferred_element_type=jnp.float32)
        * 0.125
    )
    peak = jnp.max(scores, -1, keepdims=True)
    log_total = peak + jnp.log(jnp.sum(jnp.exp(scores - peak), -1, keepdims=True))
    probs = jnp.exp(scores - log_total)
    attended = jnp.einsum(
        "bhqk,bkhd->bqhd",
        probs.astype(jnp.bfloat16),
        value_heads,
        preferred_element_type=jnp.float32,
    )
    attended = attended.reshape(rows, width).astype(jnp.bfloat16)
    residual = inputs_f + jnp.dot(attended, full_out, preferred_element_type=jnp.float32)
    normed_two, inverse_two = standardize(residual)
    second = (normed_two * full_two.astype(jnp.float32)).astype(jnp.bfloat16)
    gate_val = jnp.dot(second, full_gate, preferred_element_type=jnp.float32)
    up_val = jnp.dot(second, full_up, preferred_element_type=jnp.float32)
    hidden = (jax.nn.gelu(gate_val, approximate=False) * up_val).astype(jnp.bfloat16)
    outcome = residual + jnp.dot(hidden, full_down, preferred_element_type=jnp.float32)
    grad_top = cotangent.astype(jnp.float32).reshape(rows, width)
    grad_low = grad_top.astype(jnp.bfloat16)
    grad_hidden = against(grad_low, full_down)
    activated, gelu_pull = jax.vjp(
        lambda pre_act: jax.nn.gelu(pre_act, approximate=False), gate_val
    )
    grad_gate = gelu_pull(grad_hidden * up_val)[0].astype(jnp.bfloat16)
    grad_up = (grad_hidden * activated).astype(jnp.bfloat16)
    grad_second = against(grad_gate, full_gate) + against(grad_up, full_up)
    grad_resid, part_two = norm_back(
        grad_second, normed_two, inverse_two, full_two.astype(jnp.float32)
    )
    grad_resid = grad_resid + grad_top
    grad_proj = grad_resid.astype(jnp.bfloat16)
    grad_att = (
        against(grad_proj, full_out)
        .astype(jnp.bfloat16)
        .reshape(members, local_len, HEADS, HEAD_DIM)
    )
    scores = (
        jnp.einsum("bqhd,bkhd->bhqk", queries, key_heads, preferred_element_type=jnp.float32)
        * 0.125
    )
    probs = jnp.exp(scores - log_total)
    grad_probs = jnp.einsum(
        "bqhd,bkhd->bhqk", grad_att, value_heads, preferred_element_type=jnp.float32
    )
    row_delta = jnp.sum(grad_probs * probs, -1, keepdims=True)
    grad_scores = (probs * (grad_probs - row_delta)).astype(jnp.bfloat16)
    grad_query = (
        jnp.einsum("bhqk,bkhd->bqhd", grad_scores, key_heads, preferred_element_type=jnp.float32)
        * 0.125
    )
    value_terms = jnp.einsum(
        "bhqk,bqhd->bkhd", probs.astype(jnp.bfloat16), grad_att, preferred_element_type=jnp.float32
    )
    key_terms = (
        jnp.einsum("bhqk,bqhd->bkhd", grad_scores, queries, preferred_element_type=jnp.float32)
        * 0.125
    )
    grad_key, grad_value = (
        lax.psum_scatter(
            key_terms.reshape(members, full_len, width).astype(jnp.bfloat16),
            "ctx",
            scatter_dimension=1,
            tiled=True,
        ).astype(jnp.float32),
        lax.psum_scatter(
            value_terms.reshape(members, full_len, width).astype(jnp.bfloat16),
            "ctx",
            scatter_dimension=1,
            tiled=True,
        ).astype(jnp.float32),
    )
    grad_key = grad_key.reshape(rows, width)
    grad_value = grad_value.reshape(rows, width)
    query_pre = unturn(grad_query, cosine, sine_table).reshape(rows, width)
    key_pre = unturn(
        grad_key.reshape(members, local_len, HEADS, HEAD_DIM), cosine, sine_table
    ).reshape(rows, width)
    grad_merged = jnp.concatenate([query_pre, key_pre, grad_value], 1).astype(jnp.bfloat16)
    grad_first = against(grad_merged, full_qkv)
    grad_in, part_one = norm_back(grad_first, normed_one, inverse_one, full_one.astype(jnp.float32))
    input_grad = (grad_in + grad_resid).astype(jnp.bfloat16).reshape(members, local_len, width)
    local_grads = (
        outer_sum(first, grad_merged),
        outer_sum(attended, grad_proj),
        outer_sum(second, grad_gate),
        outer_sum(second, grad_up),
        outer_sum(grad_low, hidden),
        part_one,
        part_two,
    )
    shares = (
        lax.psum_scatter(local_grads[0], ("dp", "ctx"), scatter_dimension=0, tiled=True),
        lax.psum_scatter(local_grads[1], ("dp", "ctx"), scatter_dimension=0, tiled=True),
        lax.psum_scatter(local_grads[2], ("dp", "ctx"), scatter_dimension=0, tiled=True),
        lax.psum_scatter(local_grads[3], ("dp", "ctx"), scatter_dimension=0, tiled=True),
        lax.psum_scatter(local_grads[4], ("dp", "ctx"), scatter_dimension=0, tiled=True),
        lax.psum_scatter(local_grads[5], ("dp", "ctx"), scatter_dimension=0, tiled=True),
        lax.psum_scatter(local_grads[6], ("dp", "ctx"), scatter_dimension=0, tiled=True),
    )
    return (
        outcome.astype(jnp.bfloat16).reshape(members, local_len, width),
        input_grad,
        shares[0],
        shares[1],
        shares[2],
        shares[3],
        shares[4].T,
        shares[5],
        shares[6],
    )


BF = jnp.bfloat16
F32 = jnp.float32
BITS = ("zh", "zl", "y", "c", "x")
COORDS = pl.BlockSpec(memory_space=pltpu.SMEM)
ANY = pl.BlockSpec(memory_space=pl.ANY)


def swap(values, axis):
    return lax.ppermute(values, axis, [(0, 1), (1, 0)])


def nt(left, right):
    return lax.dot_general(left, right, (((1,), (1,)), ((), ())), preferred_element_type=F32)


def nn(left, right):
    return jnp.dot(left, right, preferred_element_type=F32)


def row_of(coords, zh, zl, y, c, x, half):
    def bit(i, flip):
        return coords[i] + flip - 2 * flip * coords[i]

    top = (bit(0, zh) * 2 + bit(1, zl)) * 2 + bit(2, y)
    row = ((top * 2 + bit(3, c)) * 2 + bit(4, x)) * 32 + half * 16
    return pl.multiple_of(row, 16)


class Chain:
    def __init__(self, steps):
        self.steps, self.value = steps, None
        self.waiting = next(steps)

    def go(self, *beside):
        ready = self.waiting
        if beside:
            tied = lax.optimization_barrier((beside, ready))
            beside, ready = tied
        try:
            self.waiting = self.steps.send(ready)
        except StopIteration as stop:
            self.value = stop.value
        return beside[0] if len(beside) == 1 else beside


def cost(micros):
    return pl.CostEstimate(
        flops=int(micros * 7e8), bytes_accessed=int(micros * 1e6), transcendentals=0
    )


def gather_steps(shard):
    count, width = shard.shape
    (parts,) = yield (shard.reshape(2, 16, width),)
    (first,) = yield (jnp.stack([parts, swap(parts, "zh")]),)
    other = swap(first, "zl")
    blocks = yield tuple(
        jnp.concatenate([first[:, half], other[:, half]], 0) for half in (0, 1)
    )
    a_x = swap(blocks[0], "x")
    b_y = swap(blocks[1], "y")
    a_two, b_two = yield (
        jnp.concatenate([blocks[0], a_x], 0),
        jnp.concatenate([blocks[1], b_y], 0),
    )
    mine = yield (a_two, swap(a_two, "y"), b_two, swap(b_two, "x"))
    return tuple(mine) + tuple(swap(piece, "c") for piece in mine)


def assemble_kernel(coords, *refs):
    out = refs[8]
    for index, piece in enumerate(refs[:8]):
        c, kind = divmod(index, 4)
        half, late = divmod(kind, 2)
        for block in range(8):
            pair, zl, zh = block // 4, (block // 2) % 2, block % 2
            x, y = (pair, late) if half == 0 else (late, pair)
            row = row_of(coords, zh, zl, y, c, x, half)
            out[pl.ds(row, 16), :] = piece[block]


def assemble(pieces, coords, width, block, start):
    return pl.pallas_call(
        assemble_kernel,
        grid=(width // block,),
        out_shape=jax.ShapeDtypeStruct((1024, width), BF),
        in_specs=[COORDS] + [pl.BlockSpec((8, 16, block), lambda j: (0, 0, start + j))] * 8,
        out_specs=pl.BlockSpec((1024, block), lambda j: (0, j)),
        cost_estimate=cost(4),
        name="assemble",
    )(coords, *pieces)


def grad_kernel(coords, x_ref, y_ref, *refs):
    keep_ref, send_ref, xt_ref, acc_ref = refs[-4:]
    j = pl.program_id(0)

    @pl.when(j == 0)
    def _():
        for i in range(4):
            rows = pl.ds(i * 256, 256)
            xt_ref[:, rows] = x_ref[rows, :].astype(F32).T.astype(BF)

    dy = y_ref[...]
    acc_ref[...] = nn(xt_ref[...], dy.reshape(dy.shape[-2:]))
    for c, out in ((0, keep_ref), (1, send_ref)):
        for block in range(32):
            half, a, b, zl, zh = [(block >> s) & 1 for s in (4, 3, 2, 1, 0)]
            y, x = (a, b) if half == 0 else (b, a)
            row = row_of(coords, zh, zl, y, c, x, half)
            out[pl.ds(block * 16, 16), :] = acc_ref[pl.ds(row, 16), :].astype(BF)


def grad_call(coords, left, right, right_spec, width, block, base, start, carry):
    steps = width // block
    out_spec = pl.BlockSpec((512, block), lambda j: (0, start + j))
    operands = [coords, left, right]
    in_specs = [COORDS, pl.BlockSpec((1024, 1024), lambda j: (0, 0)), right_spec]
    aliases = {}
    if carry is not None:
        aliases = {len(operands): 0, len(operands) + 1: 1}
        operands += list(carry)
        in_specs += [ANY, ANY]
    return pl.pallas_call(
        grad_kernel,
        grid=(steps,),
        out_shape=[jax.ShapeDtypeStruct((512, base), BF)] * 2,
        in_specs=in_specs,
        out_specs=[out_spec, out_spec],
        scratch_shapes=[pltpu.VMEM((1024, 1024), BF), pltpu.VMEM((1024, block), F32)],
        input_output_aliases=aliases,
        cost_estimate=cost(width / 230),
        name="weight_grad",
    )(*operands)


def plus(left, right):
    return (left.astype(F32) + right.astype(F32)).astype(BF)


def scatter_steps(keep, send):
    width = keep.shape[1]
    (send,) = yield (send,)
    came = swap(send, "c")

    def part(i):
        rows = slice(i * 128, (i + 1) * 128)
        return plus(keep[rows], came[rows])

    a_send, b_send = yield (part(1), part(3))
    a_got = swap(a_send, "y")
    b_got = swap(b_send, "x")
    a_keep, b_keep = part(0), part(2)
    a_next, b_next = yield (
        plus(a_keep[64:], a_got[64:]),
        plus(b_keep[64:], b_got[64:]),
    )
    a_last = swap(a_next, "x")
    b_last = swap(b_next, "y")
    a_half = plus(a_keep[:64], a_got[:64])
    b_half = plus(b_keep[:64], b_got[:64])

    def both(i):
        rows = slice(i * 32, (i + 1) * 32)
        return jnp.stack(
            [
                plus(a_half[rows], a_last[rows]).reshape(2, 16, width),
                plus(b_half[rows], b_last[rows]).reshape(2, 16, width),
            ],
            1,
        )

    (low,) = yield (both(1),)
    low_got = swap(low, "zl")
    kept = both(0)
    (high,) = yield (plus(kept[1], low_got[1]),)
    total = kept[0].astype(F32) + low_got[0].astype(F32) + swap(high, "zh").astype(F32)
    return total.reshape(32, width)


def rotated(values):
    lane = lax.broadcasted_iota(jnp.int32, values.shape, 1)
    return jnp.where((lane & 63) < 32, pltpu.roll(values, 96, 1), pltpu.roll(values, 32, 1))


def qkv_kernel(tok_ref, gain_ref, w_ref, cos_ref, sin_ref, first_ref, out_ref):
    j = pl.program_id(0)

    @pl.when(j == 0)
    def _():
        def chunk(i, carry):
            rows = pl.ds(pl.multiple_of(i * 128, 128), 128)
            normed, _ = standardize(tok_ref[rows, :].astype(F32))
            first_ref[rows, :] = (normed * gain_ref[...]).astype(BF)
            return carry

        lax.fori_loop(0, 8, chunk, 0)

    for r in range(2):
        rows = slice(r * 512, (r + 1) * 512)
        acc = nn(first_ref[rows, :], w_ref[...])

        @pl.when(j < 4)
        def _():
            scale = jnp.where(j < 2, 0.125, 1.0)
            for i in range(4):
                part = acc[:, i * 128 : (i + 1) * 128]
                turned = part * cos_ref[rows, :] + rotated(part) * sin_ref[rows, :]
                out_ref[rows, i * 128 : (i + 1) * 128] = (turned * scale).astype(BF)

        @pl.when(j >= 4)
        def _():
            out_ref[rows, :] = acc.astype(BF)


def qkv_call(rows_in, gain, w_qkv, cosine, sine):
    whole = lambda shape: pl.BlockSpec(shape, lambda j: (0, 0))
    return pl.pallas_call(
        qkv_kernel,
        grid=(6,),
        out_shape=[jax.ShapeDtypeStruct((1024, 1024), BF), jax.ShapeDtypeStruct((1024, 3072), BF)],
        in_specs=[
            whole((1024, 1024)),
            whole((1, 1024)),
            pl.BlockSpec((1024, 512), lambda j: (0, j)),
            whole((1024, 128)),
            whole((1024, 128)),
        ],
        out_specs=[whole((1024, 1024)), pl.BlockSpec((1024, 512), lambda j: (0, j))],
        cost_estimate=cost(20),
        name="norm_qkv",
    )(rows_in, gain, w_qkv, cosine, sine)


ROWS = 256


def attend_kernel(q_ref, k_ref, v_ref, *refs):
    out_ref, lse_ref = refs[-2:]
    keys, values = k_ref[...], v_ref[...]

    def chunk(i, carry):
        rows = pl.ds(pl.multiple_of(i * ROWS, ROWS), ROWS)
        q = q_ref[rows, :]
        low_half = lax.broadcasted_iota(jnp.int32, (ROWS, 128), 1) < 64
        zero = jnp.zeros_like(q)
        outs, stats = [], []
        for part in (jnp.where(low_half, q, zero), jnp.where(low_half, zero, q)):
            scores = nt(part, keys)
            peak = jnp.max(scores, -1, keepdims=True)
            weights = jnp.exp(scores - peak)
            total = jnp.sum(weights, -1, keepdims=True)
            outs.append(nn(weights.astype(BF), values) / total)
            stats.append(peak + jnp.log(total))
        out_ref[rows, :] = jnp.where(low_half, outs[0], outs[1]).astype(BF)
        lse_ref[rows, :] = jnp.where(low_half, stats[0], stats[1])
        return carry

    lax.fori_loop(0, 1024 // ROWS, chunk, 0)


def head_spec(offset):
    return pl.BlockSpec((1024, 128), lambda j: (0, offset + j))


def attend_call(qkv, start, count, carry):
    operands, in_specs, aliases = [qkv] * 3, [head_spec(i + start) for i in (0, 8, 16)], {}
    if carry is not None:
        operands += list(carry)
        in_specs += [ANY, ANY]
        aliases = {3: 0, 4: 1}
    return pl.pallas_call(
        attend_kernel,
        grid=(count,),
        out_shape=[jax.ShapeDtypeStruct((1024, 1024), BF), jax.ShapeDtypeStruct((1024, 1024), F32)],
        in_specs=in_specs,
        out_specs=[head_spec(start)] * 2,
        input_output_aliases=aliases,
        cost_estimate=cost(5 * count),
        name="attend",
    )(*operands)


def attend_back_kernel(
    q_ref, k_ref, v_ref, att_ref, lse_ref, datt_ref, cos_ref, sin_ref, *refs
):
    out_ref, qt, dt, dkt, dvt = refs[-5:]
    keys, values = k_ref[...], v_ref[...]
    lane = lax.broadcasted_iota(jnp.int32, (1024, 128), 1) < 64
    nothing = jnp.zeros_like(keys)
    key_parts = (jnp.where(lane, keys, nothing), jnp.where(lane, nothing, keys))
    for i in range(1024 // ROWS):
        rows = slice(i * ROWS, (i + 1) * ROWS)
        qt[i] = q_ref[rows, :].astype(F32).T.astype(BF)
        dt[i] = datt_ref[rows, :].astype(F32).T.astype(BF)
    dkt[...] = jnp.zeros_like(dkt)
    dvt[...] = jnp.zeros_like(dvt)

    def chunk(i, carry):
        rows = pl.ds(pl.multiple_of(i * ROWS, ROWS), ROWS)
        q, datt = q_ref[rows, :], datt_ref[rows, :]
        low_half = lax.broadcasted_iota(jnp.int32, (ROWS, 128), 1) < 64
        zero = jnp.zeros_like(q)
        mixed = datt.astype(F32) * att_ref[rows, :].astype(F32)
        grad_q = jnp.zeros((ROWS, 128), F32)
        for h in range(2):
            def pick(t, z):
                return jnp.where(low_half, t, z) if h == 0 else jnp.where(low_half, z, t)

            delta = jnp.sum(pick(mixed, jnp.zeros_like(mixed)), -1, keepdims=True)
            lse = lse_ref[rows, h * 64 : h * 64 + 1]
            probs = jnp.exp(nt(pick(q, zero), keys) - lse)
            grad_probs = nt(pick(datt, zero), values)
            grad_scores = (probs * (grad_probs - delta)).astype(BF)
            grad_q += nn(grad_scores, key_parts[h])
            side = slice(h * 64, (h + 1) * 64)
            dkt[side, :] += nn(qt[i, side, :], grad_scores)
            dvt[side, :] += nn(dt[i, side, :], probs.astype(BF))
        grad_q = grad_q * 0.125
        grad_q = grad_q * cos_ref[rows, :] - rotated(grad_q) * sin_ref[rows, :]
        out_ref[0, rows, :] = grad_q.astype(BF)
        return carry

    lax.fori_loop(0, 1024 // ROWS, chunk, 0)
    grad_k = dkt[...].T
    grad_k = grad_k * cos_ref[...] - rotated(grad_k) * sin_ref[...]
    out_ref[1] = grad_k.astype(BF)
    out_ref[2] = dvt[...].T.astype(BF)


def attend_back_call(qkv, attended, lse, datt, cosine, sine, start, count, carry):
    table = pl.BlockSpec((1024, 128), lambda j: (0, 0))
    operands = [qkv, qkv, qkv, attended, lse, datt, cosine, sine]
    in_specs = [head_spec(i + start) for i in (0, 8, 16, 0, 0, 0)] + [table] * 2
    aliases = {}
    if carry is not None:
        operands.append(carry)
        in_specs.append(ANY)
        aliases = {8: 0}
    return pl.pallas_call(
        attend_back_kernel,
        grid=(count,),
        out_shape=jax.ShapeDtypeStruct((3, 1024, 1024), BF),
        in_specs=in_specs,
        out_specs=pl.BlockSpec((3, 1024, 128), lambda j: (0, 0, start + j)),
        scratch_shapes=[
            pltpu.VMEM((1024 // ROWS, 128, ROWS), BF),
            pltpu.VMEM((1024 // ROWS, 128, ROWS), BF),
            pltpu.VMEM((128, 1024), F32),
            pltpu.VMEM((128, 1024), F32),
        ],
        input_output_aliases=aliases,
        cost_estimate=cost(7.5 * count),
        name="attend_back",
    )(*operands)


def feed_kernel(second_ref, grad_ref, gate_ref, up_ref, down_ref, hid_ref, dgate_ref, dup_ref):
    def chunk(i, carry):
        rows = pl.ds(pl.multiple_of(i * 256, 256), 256)
        second = second_ref[rows, :]
        gate = nn(second, gate_ref[...])
        up = nn(second, up_ref[...])
        grad = nn(grad_ref[rows, :], down_ref[...])
        below = 0.5 + 0.5 * lax.erf(gate * math.sqrt(0.5))
        active = gate * below
        slope = below + gate * jnp.exp(-0.5 * gate * gate) * (1.0 / math.sqrt(2.0 * math.pi))
        hid_ref[rows, :] = (active * up).astype(BF)
        dgate_ref[rows, :] = (grad * up * slope).astype(BF)
        dup_ref[rows, :] = (grad * active).astype(BF)
        return carry

    lax.fori_loop(0, 4, chunk, 0)


def feed_call(second, grad_low, w_gate, w_up, w_down_t):
    width, block = w_gate.shape[1], 896
    rows = pl.BlockSpec((1024, 1024), lambda j: (0, 0))
    cols = pl.BlockSpec((1024, block), lambda j: (0, j))
    return pl.pallas_call(
        feed_kernel,
        grid=(width // block,),
        out_shape=[jax.ShapeDtypeStruct((1024, width), BF)] * 3,
        in_specs=[rows, rows, cols, cols, cols],
        out_specs=[cols] * 3,
        cost_estimate=cost(30),
        name="feed",
    )(second, grad_low, w_gate, w_up, w_down_t)


def whole_rows(local, place):
    own = lax.dynamic_index_in_dim(local, place, 0, keepdims=False)
    got = swap(lax.dynamic_index_in_dim(local, 1 - place, 0, keepdims=False), "x")
    return jnp.where(
        place == 0, jnp.concatenate([own, got], 0), jnp.concatenate([got, own], 0)
    )


def half_rows(whole, place):
    half = whole.shape[0] // 2
    own = lax.dynamic_slice_in_dim(whole, place * half, half, 0)
    got = swap(lax.dynamic_slice_in_dim(whole, (1 - place) * half, half, 0), "x")
    return jnp.where(place == 0, jnp.stack([own, got]), jnp.stack([got, own]))


def paired_body(tokens, cotangent, w_qkv, w_out, w_gate, w_up, w_down, gain_one, gain_two):
    features = w_gate.shape[1]
    padded = -(-features // 896) * 896
    coords = jnp.stack([lax.axis_index(name) for name in BITS]).astype(jnp.int32)
    place = coords[4]
    barrier = lax.optimization_barrier

    def pad(array):
        return jnp.pad(array, ((0, 0), (0, padded - features)))

    gains = jnp.pad(jnp.stack([gain_one, gain_two], 1), ((0, 0), (0, 126)))
    shard_two = jnp.concatenate([pad(w_gate), pad(w_up), w_out], 1)
    shard_three = pad(w_down.T)
    cosine, sine = rotary_tables(1024, 0, HEAD_DIM)
    sign = jnp.where(jnp.arange(HEAD_DIM) < HEAD_DIM // 2, -1.0, 1.0)
    cosine = jnp.concatenate([cosine, cosine], 1)
    sine = jnp.concatenate([sine * sign, sine * sign], 1)

    one = Chain(gather_steps(jnp.concatenate([w_qkv, gains], 1)))
    one.go()
    rows_in = whole_rows(tokens, place)
    one.go()
    shard_two, shard_three, cotangent = one.go(shard_two, shard_three, cotangent)
    two = Chain(gather_steps(shard_two))
    two.go()
    one.go()
    two.go()
    one.go()
    full_qkv = assemble(one.value, coords, 3072, 1024, 0)
    gain_cols = assemble(one.value, coords, 128, 128, 24)
    shard_three, cotangent = two.go(shard_three, cotangent)
    three = Chain(gather_steps(shard_three))
    three.go()
    gain_rows = gain_cols[:, :2].astype(F32).T
    full_one, full_two = gain_rows[0:1], gain_rows[1:2]

    first, qkv = qkv_call(rows_in, full_one, full_qkv, cosine, sine)
    qkv = two.go(qkv)
    qkv = three.go(qkv)
    halves = attend_call(qkv, 0, 4, None)
    halves = three.go(*halves)
    halves, cotangent = barrier((halves, cotangent))
    grad_low = whole_rows(cotangent, place)
    attended, lse = attend_call(qkv, 4, 4, halves)
    attended = two.go(attended)
    attended = three.go(attended)
    full_out = assemble(two.value, coords, 1024, 256, 2 * padded // 256)
    full_gate = assemble(two.value, coords, padded, 896, 0)
    full_up = assemble(two.value, coords, padded, 896, padded // 896)

    inputs_f = rows_in.astype(F32)
    residual = inputs_f + nn(attended, full_out)
    normed_two, inverse_two = standardize(residual)
    second = (normed_two * full_two).astype(BF)
    second = three.go(second)
    full_down = assemble(three.value, coords, padded, 896, 0)
    hidden, d_gate, d_up = feed_call(second, grad_low, full_gate, full_up, full_down)

    block = 896
    col_spec = pl.BlockSpec((1024, block), lambda j: (0, j))
    per = padded // block

    def grad_of(left, right, start, total, carry):
        return grad_call(coords, left, right, col_spec, padded, block, total, start, carry)

    down = Chain(scatter_steps(*grad_of(grad_low, hidden, 0, padded, None)))
    d_gate = down.go(d_gate)
    sums = grad_of(second, d_gate, 0, 2 * padded, None)
    sums, d_up = down.go(sums, d_up)
    sums = grad_of(second, d_up, per, 2 * padded, sums)
    feed = Chain(scatter_steps(*sums))
    d_gate = feed.go(d_gate)
    d_gate = down.go(d_gate)
    grad_second = nt(d_gate, full_gate)
    grad_second, d_up = feed.go(grad_second, d_up)
    grad_second, d_up = down.go(grad_second, d_up)
    grad_second = grad_second + nt(d_up, full_up)
    grad_resid, part_two = norm_back(grad_second, normed_two, inverse_two, full_two)
    grad_resid = grad_resid + grad_low.astype(F32)
    grad_proj = grad_resid.astype(BF)
    grad_proj = down.go(grad_proj)
    datt = nt(grad_proj, full_out).astype(BF)
    out_spec = pl.BlockSpec((1024, 512), lambda j: (0, j))
    out = Chain(
        scatter_steps(*grad_call(coords, attended, grad_proj, out_spec, 1024, 512, 1024, 0, None))
    )
    datt = out.go(datt)
    fused = attend_back_call(qkv, attended, lse, datt, cosine, sine, 0, 2, None)
    fused = feed.go(fused)
    fused = out.go(fused)
    fused = attend_back_call(qkv, attended, lse, datt, cosine, sine, 2, 2, fused)
    fused = feed.go(fused)
    fused = out.go(fused)
    outcome = (residual + nt(hidden, full_down)).astype(BF)
    fused, outcome = barrier((fused, outcome))
    result = half_rows(outcome, place)
    fused = attend_back_call(qkv, attended, lse, datt, cosine, sine, 4, 2, fused)
    fused = feed.go(fused)
    fused = out.go(fused)
    fused = attend_back_call(qkv, attended, lse, datt, cosine, sine, 6, 2, fused)
    fused = out.go(fused)

    qkv_spec = pl.BlockSpec((1, 1024, 1024), lambda j: (j, 0, 0))
    last = Chain(
        scatter_steps(*grad_call(coords, first, fused, qkv_spec, 3072, 1024, 3072, 0, None))
    )
    fused = last.go(fused)
    grad_first = nt(fused[0], full_qkv[:, :1024])
    grad_first, fused = last.go(grad_first, fused)
    grad_first = grad_first + nt(fused[1], full_qkv[:, 1024:2048])
    grad_first = grad_first + nt(fused[2], full_qkv[:, 2048:])
    grad_first = last.go(grad_first)
    normed_one, inverse_one = standardize(inputs_f)
    grad_in, part_one = norm_back(grad_first, normed_one, inverse_one, full_one)
    input_grad = half_rows((grad_in + grad_resid).astype(BF), place)
    parts = jnp.stack([part_one, part_two])
    for axis in BITS:
        parts = parts + swap(parts, axis)
    index = ((((coords[0] * 2 + coords[1]) * 2 + coords[2]) * 2 + coords[3]) * 2 + coords[4]) * 32
    parts = lax.dynamic_slice_in_dim(parts, index, 32, 1)
    last.go()
    last.go()
    return (
        result,
        input_grad,
        last.value,
        out.value,
        feed.value[:, :features],
        feed.value[:, padded : padded + features],
        down.value[:, :features].T,
        parts[0],
        parts[1],
    )


def solution(mesh):
    groups, pair = mesh.shape["dp"], mesh.shape["ctx"]
    if (groups, pair) == (16, 2):
        mesh = jax.sharding.Mesh(mesh.devices.reshape(2, 2, 2, 2, 2), BITS)
        outer, inner, run = BITS[:4], "x", paired_body
    else:
        outer, inner, run = "dp", "ctx", body
    every = BITS if run is paired_body else ("dp", "ctx")
    whole, rows, cols, line = P(outer, inner, None), P(every, None), P(None, every), P(every)
    in_specs = (whole, whole, rows, rows, rows, rows, cols, line, line)
    out_specs = (whole, whole, rows, rows, rows, rows, cols, line, line)
    return jax.shard_map(run, mesh=mesh, in_specs=in_specs, out_specs=out_specs, check_vma=False)
```

```python
import functools
import math

import jax
import jax.numpy as jnp
from jax import lax
from jax.experimental import pallas as pl
from jax.experimental.pallas import tpu as pltpu
from jax.sharding import PartitionSpec as P

HEADS = 16
HEAD_DIM = 64


THETA = 160000.0
EPSILON = 1e-05


def rotary_tables(length, offset, head_size):
    halfway = head_size // 2
    frequency = jnp.exp(
        jnp.arange(halfway).astype(jnp.float32) * (-2.0 * math.log(THETA) / head_size)
    )
    position = (offset + jnp.arange(length)).astype(jnp.float32)
    angles = position[:, None] * frequency[None, :]
    cosine = jnp.cos(angles)
    sine_table = jnp.sin(angles)
    return (jnp.concatenate([cosine, cosine], -1), jnp.concatenate([sine_table, sine_table], -1))


def rotate_half(values):
    halfway = values.shape[-1] // 2
    return jnp.concatenate([-values[..., halfway:], values[..., :halfway]], -1)


def turn(values, cosine, sine_table):
    return values * cosine[:, None, :] + rotate_half(values) * sine_table[:, None, :]


def unturn(values, cosine, sine_table):
    return values * cosine[:, None, :] - rotate_half(values) * sine_table[:, None, :]


def standardize(values):
    centered = values - jnp.mean(values, -1, keepdims=True)
    inverse = lax.rsqrt(jnp.mean(centered * centered, -1, keepdims=True) + EPSILON)
    return (centered * inverse, inverse)


def norm_back(grad_normed, normed, inverse, gain_full):
    scaled = grad_normed * gain_full
    inner = (
        scaled
        - jnp.mean(scaled, -1, keepdims=True)
        - normed * jnp.mean(scaled * normed, -1, keepdims=True)
    )
    return (inverse * inner, jnp.sum(grad_normed * normed, 0))


def against(left, weight):
    return lax.dot_general(
        left, weight, (((1,), (1,)), ((), ())), preferred_element_type=jnp.float32
    )


def outer_sum(left, right):
    return lax.dot_general(
        left, right, (((0,), (0,)), ((), ())), preferred_element_type=jnp.float32
    )


def body(tokens, cotangent, w_qkv, w_out, w_gate, w_up, w_down, gain_one, gain_two):
    members, local_len, width = tokens.shape
    rows = members * local_len
    shards = (w_qkv, w_out, w_gate, w_up, w_down, gain_one, gain_two)
    offset = lax.axis_index("ctx") * local_len
    cosine, sine_table = rotary_tables(local_len, offset, HEAD_DIM)
    current = (
        lax.all_gather(shards[0], ("dp", "ctx"), axis=0, tiled=True),
        lax.all_gather(shards[1], ("dp", "ctx"), axis=0, tiled=True),
        lax.all_gather(shards[2], ("dp", "ctx"), axis=0, tiled=True),
        lax.all_gather(shards[3], ("dp", "ctx"), axis=0, tiled=True),
        lax.all_gather(shards[4], ("dp", "ctx"), axis=1, tiled=True),
        lax.all_gather(shards[5], ("dp", "ctx"), axis=0, tiled=True),
        lax.all_gather(shards[6], ("dp", "ctx"), axis=0, tiled=True),
    )
    full_qkv, full_out, full_gate, full_up, full_down, full_one, full_two = current
    inputs_f = tokens.astype(jnp.float32).reshape(rows, width)
    normed_one, inverse_one = standardize(inputs_f)
    first = (normed_one * full_one.astype(jnp.float32)).astype(jnp.bfloat16)
    merged = jnp.dot(first, full_qkv, preferred_element_type=jnp.float32)
    queries = turn(
        merged[:, :width].reshape(members, local_len, HEADS, HEAD_DIM), cosine, sine_table
    ).astype(jnp.bfloat16)
    key_own = turn(
        merged[:, width : 2 * width].reshape(members, local_len, HEADS, HEAD_DIM),
        cosine,
        sine_table,
    ).astype(jnp.bfloat16)
    value_own = (
        merged[:, 2 * width :].astype(jnp.bfloat16).reshape(members, local_len, HEADS, HEAD_DIM)
    )
    key_all, value_all = (
        lax.all_gather(key_own.reshape(members, local_len, width), "ctx", axis=1, tiled=True),
        lax.all_gather(value_own.reshape(members, local_len, width), "ctx", axis=1, tiled=True),
    )
    full_len = key_all.shape[1]
    key_heads = key_all.reshape(members, full_len, HEADS, HEAD_DIM)
    value_heads = value_all.reshape(members, full_len, HEADS, HEAD_DIM)
    scores = (
        jnp.einsum("bqhd,bkhd->bhqk", queries, key_heads, preferred_element_type=jnp.float32)
        * 0.125
    )
    peak = jnp.max(scores, -1, keepdims=True)
    log_total = peak + jnp.log(jnp.sum(jnp.exp(scores - peak), -1, keepdims=True))
    probs = jnp.exp(scores - log_total)
    attended = jnp.einsum(
        "bhqk,bkhd->bqhd",
        probs.astype(jnp.bfloat16),
        value_heads,
        preferred_element_type=jnp.float32,
    )
    attended = attended.reshape(rows, width).astype(jnp.bfloat16)
    residual = inputs_f + jnp.dot(attended, full_out, preferred_element_type=jnp.float32)
    normed_two, inverse_two = standardize(residual)
    second = (normed_two * full_two.astype(jnp.float32)).astype(jnp.bfloat16)
    gate_val = jnp.dot(second, full_gate, preferred_element_type=jnp.float32)
    up_val = jnp.dot(second, full_up, preferred_element_type=jnp.float32)
    hidden = (jax.nn.gelu(gate_val, approximate=False) * up_val).astype(jnp.bfloat16)
    outcome = residual + jnp.dot(hidden, full_down, preferred_element_type=jnp.float32)
    grad_top = cotangent.astype(jnp.float32).reshape(rows, width)
    grad_low = grad_top.astype(jnp.bfloat16)
    grad_hidden = against(grad_low, full_down)
    activated, gelu_pull = jax.vjp(
        lambda pre_act: jax.nn.gelu(pre_act, approximate=False), gate_val
    )
    grad_gate = gelu_pull(grad_hidden * up_val)[0].astype(jnp.bfloat16)
    grad_up = (grad_hidden * activated).astype(jnp.bfloat16)
    grad_second = against(grad_gate, full_gate) + against(grad_up, full_up)
    grad_resid, part_two = norm_back(
        grad_second, normed_two, inverse_two, full_two.astype(jnp.float32)
    )
    grad_resid = grad_resid + grad_top
    grad_proj = grad_resid.astype(jnp.bfloat16)
    grad_att = (
        against(grad_proj, full_out)
        .astype(jnp.bfloat16)
        .reshape(members, local_len, HEADS, HEAD_DIM)
    )
    scores = (
        jnp.einsum("bqhd,bkhd->bhqk", queries, key_heads, preferred_element_type=jnp.float32)
        * 0.125
    )
    probs = jnp.exp(scores - log_total)
    grad_probs = jnp.einsum(
        "bqhd,bkhd->bhqk", grad_att, value_heads, preferred_element_type=jnp.float32
    )
    row_delta = jnp.sum(grad_probs * probs, -1, keepdims=True)
    grad_scores = (probs * (grad_probs - row_delta)).astype(jnp.bfloat16)
    grad_query = (
        jnp.einsum("bhqk,bkhd->bqhd", grad_scores, key_heads, preferred_element_type=jnp.float32)
        * 0.125
    )
    value_terms = jnp.einsum(
        "bhqk,bqhd->bkhd", probs.astype(jnp.bfloat16), grad_att, preferred_element_type=jnp.float32
    )
    key_terms = (
        jnp.einsum("bhqk,bqhd->bkhd", grad_scores, queries, preferred_element_type=jnp.float32)
        * 0.125
    )
    grad_key, grad_value = (
        lax.psum_scatter(
            key_terms.reshape(members, full_len, width).astype(jnp.bfloat16),
            "ctx",
            scatter_dimension=1,
            tiled=True,
        ).astype(jnp.float32),
        lax.psum_scatter(
            value_terms.reshape(members, full_len, width).astype(jnp.bfloat16),
            "ctx",
            scatter_dimension=1,
            tiled=True,
        ).astype(jnp.float32),
    )
    grad_key = grad_key.reshape(rows, width)
    grad_value = grad_value.reshape(rows, width)
    query_pre = unturn(grad_query, cosine, sine_table).reshape(rows, width)
    key_pre = unturn(
        grad_key.reshape(members, local_len, HEADS, HEAD_DIM), cosine, sine_table
    ).reshape(rows, width)
    grad_merged = jnp.concatenate([query_pre, key_pre, grad_value], 1).astype(jnp.bfloat16)
    grad_first = against(grad_merged, full_qkv)
    grad_in, part_one = norm_back(grad_first, normed_one, inverse_one, full_one.astype(jnp.float32))
    input_grad = (grad_in + grad_resid).astype(jnp.bfloat16).reshape(members, local_len, width)
    local_grads = (
        outer_sum(first, grad_merged),
        outer_sum(attended, grad_proj),
        outer_sum(second, grad_gate),
        outer_sum(second, grad_up),
        outer_sum(grad_low, hidden),
        part_one,
        part_two,
    )
    shares = (
        lax.psum_scatter(local_grads[0], ("dp", "ctx"), scatter_dimension=0, tiled=True),
        lax.psum_scatter(local_grads[1], ("dp", "ctx"), scatter_dimension=0, tiled=True),
        lax.psum_scatter(local_grads[2], ("dp", "ctx"), scatter_dimension=0, tiled=True),
        lax.psum_scatter(local_grads[3], ("dp", "ctx"), scatter_dimension=0, tiled=True),
        lax.psum_scatter(local_grads[4], ("dp", "ctx"), scatter_dimension=0, tiled=True),
        lax.psum_scatter(local_grads[5], ("dp", "ctx"), scatter_dimension=0, tiled=True),
        lax.psum_scatter(local_grads[6], ("dp", "ctx"), scatter_dimension=0, tiled=True),
    )
    return (
        outcome.astype(jnp.bfloat16).reshape(members, local_len, width),
        input_grad,
        shares[0],
        shares[1],
        shares[2],
        shares[3],
        shares[4].T,
        shares[5],
        shares[6],
    )


BF = jnp.bfloat16
F32 = jnp.float32
BITS = ("zh", "zl", "y", "c", "x")
COORDS = pl.BlockSpec(memory_space=pltpu.SMEM)
ANY = pl.BlockSpec(memory_space=pl.ANY)


def swap(values, axis):
    return lax.ppermute(values, axis, [(0, 1), (1, 0)])


def nt(left, right):
    return lax.dot_general(left, right, (((1,), (1,)), ((), ())), preferred_element_type=F32)


def nn(left, right):
    return jnp.dot(left, right, preferred_element_type=F32)


def row_of(coords, zh, zl, y, c, x, half):
    def bit(i, flip):
        return coords[i] + flip - 2 * flip * coords[i]

    top = (bit(0, zh) * 2 + bit(1, zl)) * 2 + bit(2, y)
    row = ((top * 2 + bit(3, c)) * 2 + bit(4, x)) * 32 + half * 16
    return pl.multiple_of(row, 16)


class Chain:
    def __init__(self, steps):
        self.steps, self.value = steps, None
        self.waiting = next(steps)

    def go(self, *beside):
        ready = self.waiting
        if beside:
            tied = lax.optimization_barrier((beside, ready))
            beside, ready = tied
        try:
            self.waiting = self.steps.send(ready)
        except StopIteration as stop:
            self.value = stop.value
        return beside[0] if len(beside) == 1 else beside


def cost(micros):
    return pl.CostEstimate(
        flops=int(micros * 7e8), bytes_accessed=int(micros * 1e6), transcendentals=0
    )


def gather_steps(shard):
    count, width = shard.shape
    (parts,) = yield (shard.reshape(2, 16, width),)
    (first,) = yield (jnp.stack([parts, swap(parts, "zh")]),)
    other = swap(first, "zl")
    blocks = yield tuple(
        jnp.concatenate([first[:, half], other[:, half]], 0) for half in (0, 1)
    )
    a_x = swap(blocks[0], "x")
    b_y = swap(blocks[1], "y")
    a_two, b_two = yield (
        jnp.concatenate([blocks[0], a_x], 0),
        jnp.concatenate([blocks[1], b_y], 0),
    )
    mine = yield (a_two, swap(a_two, "y"), b_two, swap(b_two, "x"))
    return tuple(mine) + tuple(swap(piece, "c") for piece in mine)


def assemble_kernel(coords, *refs):
    out = refs[8]
    for index, piece in enumerate(refs[:8]):
        c, kind = divmod(index, 4)
        half, late = divmod(kind, 2)
        for block in range(8):
            pair, zl, zh = block // 4, (block // 2) % 2, block % 2
            x, y = (pair, late) if half == 0 else (late, pair)
            row = row_of(coords, zh, zl, y, c, x, half)
            out[pl.ds(row, 16), :] = piece[block]


def assemble(pieces, coords, width, block, start):
    return pl.pallas_call(
        assemble_kernel,
        grid=(width // block,),
        out_shape=jax.ShapeDtypeStruct((1024, width), BF),
        in_specs=[COORDS] + [pl.BlockSpec((8, 16, block), lambda j: (0, 0, start + j))] * 8,
        out_specs=pl.BlockSpec((1024, block), lambda j: (0, j)),
        cost_estimate=cost(4),
        name="assemble",
    )(coords, *pieces)


def grad_kernel(coords, x_ref, y_ref, *refs):
    keep_ref, send_ref, xt_ref, acc_ref = refs[-4:]
    j = pl.program_id(0)

    @pl.when(j == 0)
    def _():
        for i in range(4):
            rows = pl.ds(i * 256, 256)
            xt_ref[:, rows] = x_ref[rows, :].astype(F32).T.astype(BF)

    dy = y_ref[...]
    acc_ref[...] = nn(xt_ref[...], dy.reshape(dy.shape[-2:]))
    for c, out in ((0, keep_ref), (1, send_ref)):
        for block in range(32):
            half, a, b, zl, zh = [(block >> s) & 1 for s in (4, 3, 2, 1, 0)]
            y, x = (a, b) if half == 0 else (b, a)
            row = row_of(coords, zh, zl, y, c, x, half)
            out[pl.ds(block * 16, 16), :] = acc_ref[pl.ds(row, 16), :].astype(BF)


def grad_call(coords, left, right, right_spec, width, block, base, start, carry):
    steps = width // block
    out_spec = pl.BlockSpec((512, block), lambda j: (0, start + j))
    operands = [coords, left, right]
    in_specs = [COORDS, pl.BlockSpec((1024, 1024), lambda j: (0, 0)), right_spec]
    aliases = {}
    if carry is not None:
        aliases = {len(operands): 0, len(operands) + 1: 1}
        operands += list(carry)
        in_specs += [ANY, ANY]
    return pl.pallas_call(
        grad_kernel,
        grid=(steps,),
        out_shape=[jax.ShapeDtypeStruct((512, base), BF)] * 2,
        in_specs=in_specs,
        out_specs=[out_spec, out_spec],
        scratch_shapes=[pltpu.VMEM((1024, 1024), BF), pltpu.VMEM((1024, block), F32)],
        input_output_aliases=aliases,
        cost_estimate=cost(width / 230),
        name="weight_grad",
    )(*operands)


def plus(left, right):
    return (left.astype(F32) + right.astype(F32)).astype(BF)


def scatter_steps(keep, send):
    width = keep.shape[1]
    (send,) = yield (send,)
    came = swap(send, "c")

    def part(i):
        rows = slice(i * 128, (i + 1) * 128)
        return plus(keep[rows], came[rows])

    a_send, b_send = yield (part(1), part(3))
    a_got = swap(a_send, "y")
    b_got = swap(b_send, "x")
    a_keep, b_keep = part(0), part(2)
    a_next, b_next = yield (
        plus(a_keep[64:], a_got[64:]),
        plus(b_keep[64:], b_got[64:]),
    )
    a_last = swap(a_next, "x")
    b_last = swap(b_next, "y")
    a_half = plus(a_keep[:64], a_got[:64])
    b_half = plus(b_keep[:64], b_got[:64])

    def both(i):
        rows = slice(i * 32, (i + 1) * 32)
        return jnp.stack(
            [
                plus(a_half[rows], a_last[rows]).reshape(2, 16, width),
                plus(b_half[rows], b_last[rows]).reshape(2, 16, width),
            ],
            1,
        )

    (low,) = yield (both(1),)
    low_got = swap(low, "zl")
    kept = both(0)
    (high,) = yield (plus(kept[1], low_got[1]),)
    total = kept[0].astype(F32) + low_got[0].astype(F32) + swap(high, "zh").astype(F32)
    return total.reshape(32, width)


def rotated(values):
    lane = lax.broadcasted_iota(jnp.int32, values.shape, 1)
    return jnp.where((lane & 63) < 32, pltpu.roll(values, 96, 1), pltpu.roll(values, 32, 1))


def qkv_kernel(tok_ref, gain_ref, w_ref, cos_ref, sin_ref, first_ref, out_ref):
    j = pl.program_id(0)

    @pl.when(j == 0)
    def _():
        def chunk(i, carry):
            rows = pl.ds(pl.multiple_of(i * 128, 128), 128)
            normed, _ = standardize(tok_ref[rows, :].astype(F32))
            first_ref[rows, :] = (normed * gain_ref[...]).astype(BF)
            return carry

        lax.fori_loop(0, 8, chunk, 0)

    for r in range(2):
        rows = slice(r * 512, (r + 1) * 512)
        acc = nn(first_ref[rows, :], w_ref[...])

        @pl.when(j < 4)
        def _():
            scale = jnp.where(j < 2, 0.125, 1.0)
            for i in range(4):
                part = acc[:, i * 128 : (i + 1) * 128]
                turned = part * cos_ref[rows, :] + rotated(part) * sin_ref[rows, :]
                out_ref[rows, i * 128 : (i + 1) * 128] = (turned * scale).astype(BF)

        @pl.when(j >= 4)
        def _():
            out_ref[rows, :] = acc.astype(BF)


def qkv_call(rows_in, gain, w_qkv, cosine, sine):
    whole = lambda shape: pl.BlockSpec(shape, lambda j: (0, 0))
    return pl.pallas_call(
        qkv_kernel,
        grid=(6,),
        out_shape=[jax.ShapeDtypeStruct((1024, 1024), BF), jax.ShapeDtypeStruct((1024, 3072), BF)],
        in_specs=[
            whole((1024, 1024)),
            whole((1, 1024)),
            pl.BlockSpec((1024, 512), lambda j: (0, j)),
            whole((1024, 128)),
            whole((1024, 128)),
        ],
        out_specs=[whole((1024, 1024)), pl.BlockSpec((1024, 512), lambda j: (0, j))],
        cost_estimate=cost(20),
        name="norm_qkv",
    )(rows_in, gain, w_qkv, cosine, sine)


ROWS = 256


def attend_kernel(q_ref, k_ref, v_ref, *refs):
    out_ref, lse_ref = refs[-2:]
    keys, values = k_ref[...], v_ref[...]

    def chunk(i, carry):
        rows = pl.ds(pl.multiple_of(i * ROWS, ROWS), ROWS)
        q = q_ref[rows, :]
        low_half = lax.broadcasted_iota(jnp.int32, (ROWS, 128), 1) < 64
        zero = jnp.zeros_like(q)
        outs, stats = [], []
        for part in (jnp.where(low_half, q, zero), jnp.where(low_half, zero, q)):
            scores = nt(part, keys)
            peak = jnp.max(scores, -1, keepdims=True)
            weights = jnp.exp(scores - peak)
            total = jnp.sum(weights, -1, keepdims=True)
            outs.append(nn(weights.astype(BF), values) / total)
            stats.append(peak + jnp.log(total))
        out_ref[rows, :] = jnp.where(low_half, outs[0], outs[1]).astype(BF)
        lse_ref[rows, :] = jnp.where(low_half, stats[0], stats[1])
        return carry

    lax.fori_loop(0, 1024 // ROWS, chunk, 0)


def head_spec(offset):
    return pl.BlockSpec((1024, 128), lambda j: (0, offset + j))


def attend_call(qkv, start, count, carry):
    operands, in_specs, aliases = [qkv] * 3, [head_spec(i + start) for i in (0, 8, 16)], {}
    if carry is not None:
        operands += list(carry)
        in_specs += [ANY, ANY]
        aliases = {3: 0, 4: 1}
    return pl.pallas_call(
        attend_kernel,
        grid=(count,),
        out_shape=[jax.ShapeDtypeStruct((1024, 1024), BF), jax.ShapeDtypeStruct((1024, 1024), F32)],
        in_specs=in_specs,
        out_specs=[head_spec(start)] * 2,
        input_output_aliases=aliases,
        cost_estimate=cost(5 * count),
        name="attend",
    )(*operands)


def attend_back_kernel(
    q_ref, k_ref, v_ref, att_ref, lse_ref, datt_ref, cos_ref, sin_ref, *refs
):
    out_ref, qt, dt, dkt, dvt = refs[-5:]
    keys, values = k_ref[...], v_ref[...]
    lane = lax.broadcasted_iota(jnp.int32, (1024, 128), 1) < 64
    nothing = jnp.zeros_like(keys)
    key_parts = (jnp.where(lane, keys, nothing), jnp.where(lane, nothing, keys))
    for i in range(1024 // ROWS):
        rows = slice(i * ROWS, (i + 1) * ROWS)
        qt[i] = q_ref[rows, :].astype(F32).T.astype(BF)
        dt[i] = datt_ref[rows, :].astype(F32).T.astype(BF)
    dkt[...] = jnp.zeros_like(dkt)
    dvt[...] = jnp.zeros_like(dvt)

    def chunk(i, carry):
        rows = pl.ds(pl.multiple_of(i * ROWS, ROWS), ROWS)
        q, datt = q_ref[rows, :], datt_ref[rows, :]
        low_half = lax.broadcasted_iota(jnp.int32, (ROWS, 128), 1) < 64
        zero = jnp.zeros_like(q)
        mixed = datt.astype(F32) * att_ref[rows, :].astype(F32)
        grad_q = jnp.zeros((ROWS, 128), F32)
        for h in range(2):
            def pick(t, z):
                return jnp.where(low_half, t, z) if h == 0 else jnp.where(low_half, z, t)

            delta = jnp.sum(pick(mixed, jnp.zeros_like(mixed)), -1, keepdims=True)
            lse = lse_ref[rows, h * 64 : h * 64 + 1]
            probs = jnp.exp(nt(pick(q, zero), keys) - lse)
            grad_probs = nt(pick(datt, zero), values)
            grad_scores = (probs * (grad_probs - delta)).astype(BF)
            grad_q += nn(grad_scores, key_parts[h])
            side = slice(h * 64, (h + 1) * 64)
            dkt[side, :] += nn(qt[i, side, :], grad_scores)
            dvt[side, :] += nn(dt[i, side, :], probs.astype(BF))
        grad_q = grad_q * 0.125
        grad_q = grad_q * cos_ref[rows, :] - rotated(grad_q) * sin_ref[rows, :]
        out_ref[0, rows, :] = grad_q.astype(BF)
        return carry

    lax.fori_loop(0, 1024 // ROWS, chunk, 0)
    grad_k = dkt[...].T
    grad_k = grad_k * cos_ref[...] - rotated(grad_k) * sin_ref[...]
    out_ref[1] = grad_k.astype(BF)
    out_ref[2] = dvt[...].T.astype(BF)


def attend_back_call(qkv, attended, lse, datt, cosine, sine, start, count, carry):
    table = pl.BlockSpec((1024, 128), lambda j: (0, 0))
    operands = [qkv, qkv, qkv, attended, lse, datt, cosine, sine]
    in_specs = [head_spec(i + start) for i in (0, 8, 16, 0, 0, 0)] + [table] * 2
    aliases = {}
    if carry is not None:
        operands.append(carry)
        in_specs.append(ANY)
        aliases = {8: 0}
    return pl.pallas_call(
        attend_back_kernel,
        grid=(count,),
        out_shape=jax.ShapeDtypeStruct((3, 1024, 1024), BF),
        in_specs=in_specs,
        out_specs=pl.BlockSpec((3, 1024, 128), lambda j: (0, 0, start + j)),
        scratch_shapes=[
            pltpu.VMEM((1024 // ROWS, 128, ROWS), BF),
            pltpu.VMEM((1024 // ROWS, 128, ROWS), BF),
            pltpu.VMEM((128, 1024), F32),
            pltpu.VMEM((128, 1024), F32),
        ],
        input_output_aliases=aliases,
        cost_estimate=cost(7.5 * count),
        name="attend_back",
    )(*operands)


def feed_kernel(second_ref, grad_ref, gate_ref, up_ref, down_ref, hid_ref, dgate_ref, dup_ref):
    def chunk(i, carry):
        rows = pl.ds(pl.multiple_of(i * 256, 256), 256)
        second = second_ref[rows, :]
        gate = nn(second, gate_ref[...])
        up = nn(second, up_ref[...])
        grad = nn(grad_ref[rows, :], down_ref[...])
        below = 0.5 + 0.5 * lax.erf(gate * math.sqrt(0.5))
        active = gate * below
        slope = below + gate * jnp.exp(-0.5 * gate * gate) * (1.0 / math.sqrt(2.0 * math.pi))
        hid_ref[rows, :] = (active * up).astype(BF)
        dgate_ref[rows, :] = (grad * up * slope).astype(BF)
        dup_ref[rows, :] = (grad * active).astype(BF)
        return carry

    lax.fori_loop(0, 4, chunk, 0)


def feed_call(second, grad_low, w_gate, w_up, w_down_t):
    width, block = w_gate.shape[1], 896
    rows = pl.BlockSpec((1024, 1024), lambda j: (0, 0))
    cols = pl.BlockSpec((1024, block), lambda j: (0, j))
    return pl.pallas_call(
        feed_kernel,
        grid=(width // block,),
        out_shape=[jax.ShapeDtypeStruct((1024, width), BF)] * 3,
        in_specs=[rows, rows, cols, cols, cols],
        out_specs=[cols] * 3,
        cost_estimate=cost(30),
        name="feed",
    )(second, grad_low, w_gate, w_up, w_down_t)


def whole_rows(local, place):
    own = lax.dynamic_index_in_dim(local, place, 0, keepdims=False)
    got = swap(lax.dynamic_index_in_dim(local, 1 - place, 0, keepdims=False), "x")
    return jnp.where(
        place == 0, jnp.concatenate([own, got], 0), jnp.concatenate([got, own], 0)
    )


def half_rows(whole, place):
    half = whole.shape[0] // 2
    own = lax.dynamic_slice_in_dim(whole, place * half, half, 0)
    got = swap(lax.dynamic_slice_in_dim(whole, (1 - place) * half, half, 0), "x")
    return jnp.where(place == 0, jnp.stack([own, got]), jnp.stack([got, own]))


def paired_body(tokens, cotangent, w_qkv, w_out, w_gate, w_up, w_down, gain_one, gain_two):
    features = w_gate.shape[1]
    padded = -(-features // 896) * 896
    coords = jnp.stack([lax.axis_index(name) for name in BITS]).astype(jnp.int32)
    place = coords[4]
    barrier = lax.optimization_barrier

    def pad(array):
        return jnp.pad(array, ((0, 0), (0, padded - features)))

    gains = jnp.pad(jnp.stack([gain_one, gain_two], 1), ((0, 0), (0, 126)))
    shard_two = jnp.concatenate([pad(w_gate), pad(w_up), w_out], 1)
    shard_three = pad(w_down.T)
    cosine, sine = rotary_tables(1024, 0, HEAD_DIM)
    sign = jnp.where(jnp.arange(HEAD_DIM) < HEAD_DIM // 2, -1.0, 1.0)
    cosine = jnp.concatenate([cosine, cosine], 1)
    sine = jnp.concatenate([sine * sign, sine * sign], 1)

    one = Chain(gather_steps(jnp.concatenate([w_qkv, gains], 1)))
    one.go()
    rows_in = whole_rows(tokens, place)
    one.go()
    shard_two = one.go(shard_two)
    two = Chain(gather_steps(shard_two))
    two.go()
    one.go()
    cotangent, two.waiting = one.go(cotangent, two.waiting)
    grad_low = whole_rows(cotangent, place)
    two.go()
    full_qkv = assemble(one.value, coords, 3072, 1024, 0)
    gain_cols = assemble(one.value, coords, 128, 128, 24)
    full_qkv, shard_three = two.go(full_qkv, shard_three)
    three = Chain(gather_steps(shard_three))
    three.go()
    gain_rows = gain_cols[:, :2].astype(F32).T
    full_one, full_two = gain_rows[0:1], gain_rows[1:2]

    first, qkv = qkv_call(rows_in, full_one, full_qkv, cosine, sine)
    qkv = two.go(qkv)
    qkv = three.go(qkv)
    halves = attend_call(qkv, 0, 3, None)
    halves = three.go(*halves)
    halves = attend_call(qkv, 3, 4, halves)
    halves = three.go(*halves)
    attended, lse = attend_call(qkv, 7, 1, halves)
    attended = two.go(attended)
    full_out = assemble(two.value, coords, 1024, 256, 2 * padded // 256)
    full_gate = assemble(two.value, coords, padded, 896, 0)
    full_up = assemble(two.value, coords, padded, 896, padded // 896)

    inputs_f = rows_in.astype(F32)
    residual = inputs_f + nn(attended, full_out)
    normed_two, inverse_two = standardize(residual)
    second = (normed_two * full_two).astype(BF)
    second = three.go(second)
    full_down = assemble(three.value, coords, padded, 896, 0)
    hidden, d_gate, d_up = feed_call(second, grad_low, full_gate, full_up, full_down)

    block = 896
    col_spec = pl.BlockSpec((1024, block), lambda j: (0, j))
    per = padded // block

    def grad_of(left, right, start, total, carry):
        return grad_call(coords, left, right, col_spec, padded, block, total, start, carry)

    down = Chain(scatter_steps(*grad_of(grad_low, hidden, 0, padded, None)))
    d_gate = down.go(d_gate)
    sums = grad_of(second, d_gate, 0, 2 * padded, None)
    sums, d_up = down.go(sums, d_up)
    sums = grad_of(second, d_up, per, 2 * padded, sums)
    feed = Chain(scatter_steps(*sums))
    d_gate = feed.go(d_gate)
    d_gate = down.go(d_gate)
    grad_second = nt(d_gate, full_gate)
    grad_second, d_up = feed.go(grad_second, d_up)
    grad_second = grad_second + nt(d_up, full_up)
    grad_resid, part_two = norm_back(grad_second, normed_two, inverse_two, full_two)
    grad_resid = grad_resid + grad_low.astype(F32)
    grad_proj = grad_resid.astype(BF)
    grad_proj = down.go(grad_proj)
    datt = nt(grad_proj, full_out).astype(BF)
    out_spec = pl.BlockSpec((1024, 512), lambda j: (0, j))
    out = Chain(
        scatter_steps(*grad_call(coords, attended, grad_proj, out_spec, 1024, 512, 1024, 0, None))
    )
    datt = out.go(datt)
    datt = down.go(datt)
    fused = attend_back_call(qkv, attended, lse, datt, cosine, sine, 0, 2, None)
    fused = feed.go(fused)
    fused = out.go(fused)
    fused = attend_back_call(qkv, attended, lse, datt, cosine, sine, 2, 2, fused)
    fused = feed.go(fused)
    fused = out.go(fused)
    outcome = (residual + nt(hidden, full_down)).astype(BF)
    fused, outcome = barrier((fused, outcome))
    result = half_rows(outcome, place)
    fused = attend_back_call(qkv, attended, lse, datt, cosine, sine, 4, 2, fused)
    fused = feed.go(fused)
    fused = out.go(fused)
    fused = attend_back_call(qkv, attended, lse, datt, cosine, sine, 6, 2, fused)
    fused = out.go(fused)

    qkv_spec = pl.BlockSpec((1, 1024, 1024), lambda j: (j, 0, 0))
    last = Chain(
        scatter_steps(*grad_call(coords, first, fused, qkv_spec, 3072, 1024, 3072, 0, None))
    )
    fused = last.go(fused)
    grad_first = nt(fused[0], full_qkv[:, :1024])
    grad_first, fused = last.go(grad_first, fused)
    grad_first = grad_first + nt(fused[1], full_qkv[:, 1024:2048])
    grad_first = grad_first + nt(fused[2], full_qkv[:, 2048:])
    grad_first = last.go(grad_first)
    normed_one, inverse_one = standardize(inputs_f)
    grad_in, part_one = norm_back(grad_first, normed_one, inverse_one, full_one)
    input_grad = half_rows((grad_in + grad_resid).astype(BF), place)
    parts = jnp.stack([part_one, part_two])
    for axis in BITS:
        parts = parts + swap(parts, axis)
    index = ((((coords[0] * 2 + coords[1]) * 2 + coords[2]) * 2 + coords[3]) * 2 + coords[4]) * 32
    parts = lax.dynamic_slice_in_dim(parts, index, 32, 1)
    last.go()
    last.go()
    return (
        result,
        input_grad,
        last.value,
        out.value,
        feed.value[:, :features],
        feed.value[:, padded : padded + features],
        down.value[:, :features].T,
        parts[0],
        parts[1],
    )


def solution(mesh):
    groups, pair = mesh.shape["dp"], mesh.shape["ctx"]
    if (groups, pair) == (16, 2):
        mesh = jax.sharding.Mesh(mesh.devices.reshape(2, 2, 2, 2, 2), BITS)
        outer, inner, run = BITS[:4], "x", paired_body
    else:
        outer, inner, run = "dp", "ctx", body
    every = BITS if run is paired_body else ("dp", "ctx")
    whole, rows, cols, line = P(outer, inner, None), P(every, None), P(None, every), P(every)
    in_specs = (whole, whole, rows, rows, rows, rows, cols, line, line)
    out_specs = (whole, whole, rows, rows, rows, rows, cols, line, line)
    return jax.shard_map(run, mesh=mesh, in_specs=in_specs, out_specs=out_specs, check_vma=False)
```

```python
import functools
import math

import jax
import jax.numpy as jnp
from jax import lax
from jax.experimental import pallas as pl
from jax.experimental.pallas import tpu as pltpu
from jax.sharding import PartitionSpec as P

HEADS = 16
HEAD_DIM = 64


THETA = 160000.0
EPSILON = 1e-05


def rotary_tables(length, offset, head_size):
    halfway = head_size // 2
    frequency = jnp.exp(
        jnp.arange(halfway).astype(jnp.float32) * (-2.0 * math.log(THETA) / head_size)
    )
    position = (offset + jnp.arange(length)).astype(jnp.float32)
    angles = position[:, None] * frequency[None, :]
    cosine = jnp.cos(angles)
    sine_table = jnp.sin(angles)
    return (jnp.concatenate([cosine, cosine], -1), jnp.concatenate([sine_table, sine_table], -1))


def rotate_half(values):
    halfway = values.shape[-1] // 2
    return jnp.concatenate([-values[..., halfway:], values[..., :halfway]], -1)


def turn(values, cosine, sine_table):
    return values * cosine[:, None, :] + rotate_half(values) * sine_table[:, None, :]


def unturn(values, cosine, sine_table):
    return values * cosine[:, None, :] - rotate_half(values) * sine_table[:, None, :]


def standardize(values):
    centered = values - jnp.mean(values, -1, keepdims=True)
    inverse = lax.rsqrt(jnp.mean(centered * centered, -1, keepdims=True) + EPSILON)
    return (centered * inverse, inverse)


def norm_back(grad_normed, normed, inverse, gain_full):
    scaled = grad_normed * gain_full
    inner = (
        scaled
        - jnp.mean(scaled, -1, keepdims=True)
        - normed * jnp.mean(scaled * normed, -1, keepdims=True)
    )
    return (inverse * inner, jnp.sum(grad_normed * normed, 0))


def against(left, weight):
    return lax.dot_general(
        left, weight, (((1,), (1,)), ((), ())), preferred_element_type=jnp.float32
    )


def outer_sum(left, right):
    return lax.dot_general(
        left, right, (((0,), (0,)), ((), ())), preferred_element_type=jnp.float32
    )


def body(tokens, cotangent, w_qkv, w_out, w_gate, w_up, w_down, gain_one, gain_two):
    members, local_len, width = tokens.shape
    rows = members * local_len
    shards = (w_qkv, w_out, w_gate, w_up, w_down, gain_one, gain_two)
    offset = lax.axis_index("ctx") * local_len
    cosine, sine_table = rotary_tables(local_len, offset, HEAD_DIM)
    current = (
        lax.all_gather(shards[0], ("dp", "ctx"), axis=0, tiled=True),
        lax.all_gather(shards[1], ("dp", "ctx"), axis=0, tiled=True),
        lax.all_gather(shards[2], ("dp", "ctx"), axis=0, tiled=True),
        lax.all_gather(shards[3], ("dp", "ctx"), axis=0, tiled=True),
        lax.all_gather(shards[4], ("dp", "ctx"), axis=1, tiled=True),
        lax.all_gather(shards[5], ("dp", "ctx"), axis=0, tiled=True),
        lax.all_gather(shards[6], ("dp", "ctx"), axis=0, tiled=True),
    )
    full_qkv, full_out, full_gate, full_up, full_down, full_one, full_two = current
    inputs_f = tokens.astype(jnp.float32).reshape(rows, width)
    normed_one, inverse_one = standardize(inputs_f)
    first = (normed_one * full_one.astype(jnp.float32)).astype(jnp.bfloat16)
    merged = jnp.dot(first, full_qkv, preferred_element_type=jnp.float32)
    queries = turn(
        merged[:, :width].reshape(members, local_len, HEADS, HEAD_DIM), cosine, sine_table
    ).astype(jnp.bfloat16)
    key_own = turn(
        merged[:, width : 2 * width].reshape(members, local_len, HEADS, HEAD_DIM),
        cosine,
        sine_table,
    ).astype(jnp.bfloat16)
    value_own = (
        merged[:, 2 * width :].astype(jnp.bfloat16).reshape(members, local_len, HEADS, HEAD_DIM)
    )
    key_all, value_all = (
        lax.all_gather(key_own.reshape(members, local_len, width), "ctx", axis=1, tiled=True),
        lax.all_gather(value_own.reshape(members, local_len, width), "ctx", axis=1, tiled=True),
    )
    full_len = key_all.shape[1]
    key_heads = key_all.reshape(members, full_len, HEADS, HEAD_DIM)
    value_heads = value_all.reshape(members, full_len, HEADS, HEAD_DIM)
    scores = (
        jnp.einsum("bqhd,bkhd->bhqk", queries, key_heads, preferred_element_type=jnp.float32)
        * 0.125
    )
    peak = jnp.max(scores, -1, keepdims=True)
    log_total = peak + jnp.log(jnp.sum(jnp.exp(scores - peak), -1, keepdims=True))
    probs = jnp.exp(scores - log_total)
    attended = jnp.einsum(
        "bhqk,bkhd->bqhd",
        probs.astype(jnp.bfloat16),
        value_heads,
        preferred_element_type=jnp.float32,
    )
    attended = attended.reshape(rows, width).astype(jnp.bfloat16)
    residual = inputs_f + jnp.dot(attended, full_out, preferred_element_type=jnp.float32)
    normed_two, inverse_two = standardize(residual)
    second = (normed_two * full_two.astype(jnp.float32)).astype(jnp.bfloat16)
    gate_val = jnp.dot(second, full_gate, preferred_element_type=jnp.float32)
    up_val = jnp.dot(second, full_up, preferred_element_type=jnp.float32)
    hidden = (jax.nn.gelu(gate_val, approximate=False) * up_val).astype(jnp.bfloat16)
    outcome = residual + jnp.dot(hidden, full_down, preferred_element_type=jnp.float32)
    grad_top = cotangent.astype(jnp.float32).reshape(rows, width)
    grad_low = grad_top.astype(jnp.bfloat16)
    grad_hidden = against(grad_low, full_down)
    activated, gelu_pull = jax.vjp(
        lambda pre_act: jax.nn.gelu(pre_act, approximate=False), gate_val
    )
    grad_gate = gelu_pull(grad_hidden * up_val)[0].astype(jnp.bfloat16)
    grad_up = (grad_hidden * activated).astype(jnp.bfloat16)
    grad_second = against(grad_gate, full_gate) + against(grad_up, full_up)
    grad_resid, part_two = norm_back(
        grad_second, normed_two, inverse_two, full_two.astype(jnp.float32)
    )
    grad_resid = grad_resid + grad_top
    grad_proj = grad_resid.astype(jnp.bfloat16)
    grad_att = (
        against(grad_proj, full_out)
        .astype(jnp.bfloat16)
        .reshape(members, local_len, HEADS, HEAD_DIM)
    )
    scores = (
        jnp.einsum("bqhd,bkhd->bhqk", queries, key_heads, preferred_element_type=jnp.float32)
        * 0.125
    )
    probs = jnp.exp(scores - log_total)
    grad_probs = jnp.einsum(
        "bqhd,bkhd->bhqk", grad_att, value_heads, preferred_element_type=jnp.float32
    )
    row_delta = jnp.sum(grad_probs * probs, -1, keepdims=True)
    grad_scores = (probs * (grad_probs - row_delta)).astype(jnp.bfloat16)
    grad_query = (
        jnp.einsum("bhqk,bkhd->bqhd", grad_scores, key_heads, preferred_element_type=jnp.float32)
        * 0.125
    )
    value_terms = jnp.einsum(
        "bhqk,bqhd->bkhd", probs.astype(jnp.bfloat16), grad_att, preferred_element_type=jnp.float32
    )
    key_terms = (
        jnp.einsum("bhqk,bqhd->bkhd", grad_scores, queries, preferred_element_type=jnp.float32)
        * 0.125
    )
    grad_key, grad_value = (
        lax.psum_scatter(
            key_terms.reshape(members, full_len, width).astype(jnp.bfloat16),
            "ctx",
            scatter_dimension=1,
            tiled=True,
        ).astype(jnp.float32),
        lax.psum_scatter(
            value_terms.reshape(members, full_len, width).astype(jnp.bfloat16),
            "ctx",
            scatter_dimension=1,
            tiled=True,
        ).astype(jnp.float32),
    )
    grad_key = grad_key.reshape(rows, width)
    grad_value = grad_value.reshape(rows, width)
    query_pre = unturn(grad_query, cosine, sine_table).reshape(rows, width)
    key_pre = unturn(
        grad_key.reshape(members, local_len, HEADS, HEAD_DIM), cosine, sine_table
    ).reshape(rows, width)
    grad_merged = jnp.concatenate([query_pre, key_pre, grad_value], 1).astype(jnp.bfloat16)
    grad_first = against(grad_merged, full_qkv)
    grad_in, part_one = norm_back(grad_first, normed_one, inverse_one, full_one.astype(jnp.float32))
    input_grad = (grad_in + grad_resid).astype(jnp.bfloat16).reshape(members, local_len, width)
    local_grads = (
        outer_sum(first, grad_merged),
        outer_sum(attended, grad_proj),
        outer_sum(second, grad_gate),
        outer_sum(second, grad_up),
        outer_sum(grad_low, hidden),
        part_one,
        part_two,
    )
    shares = (
        lax.psum_scatter(local_grads[0], ("dp", "ctx"), scatter_dimension=0, tiled=True),
        lax.psum_scatter(local_grads[1], ("dp", "ctx"), scatter_dimension=0, tiled=True),
        lax.psum_scatter(local_grads[2], ("dp", "ctx"), scatter_dimension=0, tiled=True),
        lax.psum_scatter(local_grads[3], ("dp", "ctx"), scatter_dimension=0, tiled=True),
        lax.psum_scatter(local_grads[4], ("dp", "ctx"), scatter_dimension=0, tiled=True),
        lax.psum_scatter(local_grads[5], ("dp", "ctx"), scatter_dimension=0, tiled=True),
        lax.psum_scatter(local_grads[6], ("dp", "ctx"), scatter_dimension=0, tiled=True),
    )
    return (
        outcome.astype(jnp.bfloat16).reshape(members, local_len, width),
        input_grad,
        shares[0],
        shares[1],
        shares[2],
        shares[3],
        shares[4].T,
        shares[5],
        shares[6],
    )


BF = jnp.bfloat16
F32 = jnp.float32
BITS = ("zh", "zl", "y", "c", "x")
COORDS = pl.BlockSpec(memory_space=pltpu.SMEM)
ANY = pl.BlockSpec(memory_space=pl.ANY)


def swap(values, axis):
    return lax.ppermute(values, axis, [(0, 1), (1, 0)])


def nt(left, right):
    return lax.dot_general(left, right, (((1,), (1,)), ((), ())), preferred_element_type=F32)


def nn(left, right):
    return jnp.dot(left, right, preferred_element_type=F32)


def row_of(coords, zh, zl, y, c, x, half):
    def bit(i, flip):
        return coords[i] + flip - 2 * flip * coords[i]

    top = (bit(0, zh) * 2 + bit(1, zl)) * 2 + bit(2, y)
    row = ((top * 2 + bit(3, c)) * 2 + bit(4, x)) * 32 + half * 16
    return pl.multiple_of(row, 16)


class Chain:
    def __init__(self, steps, ties=1):
        self.steps, self.value, self.ties = steps, None, ties
        self.waiting = next(steps)

    def go(self, *beside):
        for _ in range(self.ties):
            ready = self.waiting
            if beside:
                beside, ready = lax.optimization_barrier((beside, ready))
            try:
                self.waiting = self.steps.send(ready)
            except StopIteration as stop:
                self.value = stop.value
        return beside[0] if len(beside) == 1 else beside


def cost(micros):
    return pl.CostEstimate(
        flops=int(micros * 7e8), bytes_accessed=int(micros * 1e6), transcendentals=0
    )


def gather_steps(shard):
    count, width = shard.shape
    (parts,) = yield (shard.reshape(2, 16, width),)
    (first,) = yield (jnp.stack([parts, swap(parts, "zh")]),)
    other = swap(first, "zl")
    blocks = yield tuple(
        jnp.concatenate([first[:, half], other[:, half]], 0) for half in (0, 1)
    )
    a_x = swap(blocks[0], "x")
    b_y = swap(blocks[1], "y")
    a_two, b_two = yield (
        jnp.concatenate([blocks[0], a_x], 0),
        jnp.concatenate([blocks[1], b_y], 0),
    )
    mine = yield (a_two, swap(a_two, "y"), b_two, swap(b_two, "x"))
    return tuple(mine) + tuple(swap(piece, "c") for piece in mine)


def assemble_kernel(coords, *refs):
    out = refs[8]
    for index, piece in enumerate(refs[:8]):
        c, kind = divmod(index, 4)
        half, late = divmod(kind, 2)
        for block in range(8):
            pair, zl, zh = block // 4, (block // 2) % 2, block % 2
            x, y = (pair, late) if half == 0 else (late, pair)
            row = row_of(coords, zh, zl, y, c, x, half)
            out[pl.ds(row, 16), :] = piece[block]


def assemble(pieces, coords, width, block, start):
    return pl.pallas_call(
        assemble_kernel,
        grid=(width // block,),
        out_shape=jax.ShapeDtypeStruct((1024, width), BF),
        in_specs=[COORDS] + [pl.BlockSpec((8, 16, block), lambda j: (0, 0, start + j))] * 8,
        out_specs=pl.BlockSpec((1024, block), lambda j: (0, j)),
        cost_estimate=cost(4),
        name="assemble",
    )(coords, *pieces)


def grad_kernel(coords, x_ref, y_ref, *refs):
    keep_ref, send_ref, xt_ref, acc_ref = refs[-4:]
    j = pl.program_id(0)

    @pl.when(j == 0)
    def _():
        for i in range(4):
            rows = pl.ds(i * 256, 256)
            xt_ref[:, rows] = x_ref[rows, :].astype(F32).T.astype(BF)

    dy = y_ref[...]
    acc_ref[...] = nn(xt_ref[...], dy.reshape(dy.shape[-2:]))
    for c, out in ((0, keep_ref), (1, send_ref)):
        for block in range(32):
            half, a, b, zl, zh = [(block >> s) & 1 for s in (4, 3, 2, 1, 0)]
            y, x = (a, b) if half == 0 else (b, a)
            row = row_of(coords, zh, zl, y, c, x, half)
            out[pl.ds(block * 16, 16), :] = acc_ref[pl.ds(row, 16), :].astype(BF)


def grad_call(coords, left, right, right_spec, width, block, base, start, carry):
    steps = width // block
    out_spec = pl.BlockSpec((512, block), lambda j: (0, start + j))
    operands = [coords, left, right]
    in_specs = [COORDS, pl.BlockSpec((1024, 1024), lambda j: (0, 0)), right_spec]
    aliases = {}
    if carry is not None:
        aliases = {len(operands): 0, len(operands) + 1: 1}
        operands += list(carry)
        in_specs += [ANY, ANY]
    return pl.pallas_call(
        grad_kernel,
        grid=(steps,),
        out_shape=[jax.ShapeDtypeStruct((512, base), BF)] * 2,
        in_specs=in_specs,
        out_specs=[out_spec, out_spec],
        scratch_shapes=[pltpu.VMEM((1024, 1024), BF), pltpu.VMEM((1024, block), F32)],
        input_output_aliases=aliases,
        cost_estimate=cost(width / 230),
        name="weight_grad",
    )(*operands)


def plus(left, right):
    return (left.astype(F32) + right.astype(F32)).astype(BF)


def scatter_steps(keep, send):
    width = keep.shape[1]
    (send,) = yield (send,)
    (send,) = yield (send,)
    (came,) = yield (swap(send, "c"),)

    def part(i):
        rows = slice(i * 128, (i + 1) * 128)
        return plus(keep[rows], came[rows])

    a_send, b_send = yield (part(1), part(3))
    a_got, b_got = yield (swap(a_send, "y"), swap(b_send, "x"))
    a_keep, b_keep = part(0), part(2)
    a_next, b_next = yield (
        plus(a_keep[64:], a_got[64:]),
        plus(b_keep[64:], b_got[64:]),
    )
    a_last, b_last = yield (swap(a_next, "x"), swap(b_next, "y"))
    a_half = plus(a_keep[:64], a_got[:64])
    b_half = plus(b_keep[:64], b_got[:64])

    def both(i):
        rows = slice(i * 32, (i + 1) * 32)
        return jnp.stack(
            [
                plus(a_half[rows], a_last[rows]).reshape(2, 16, width),
                plus(b_half[rows], b_last[rows]).reshape(2, 16, width),
            ],
            1,
        )

    (low,) = yield (both(1),)
    (low_got,) = yield (swap(low, "zl"),)
    kept = both(0)
    (high,) = yield (plus(kept[1], low_got[1]),)
    total = kept[0].astype(F32) + low_got[0].astype(F32) + swap(high, "zh").astype(F32)
    return total.reshape(32, width)


def rotated(values):
    lane = lax.broadcasted_iota(jnp.int32, values.shape, 1)
    return jnp.where((lane & 63) < 32, pltpu.roll(values, 96, 1), pltpu.roll(values, 32, 1))


def qkv_kernel(tok_ref, gain_ref, w_ref, cos_ref, sin_ref, first_ref, out_ref):
    j = pl.program_id(0)

    @pl.when(j == 0)
    def _():
        def chunk(i, carry):
            rows = pl.ds(pl.multiple_of(i * 128, 128), 128)
            normed, _ = standardize(tok_ref[rows, :].astype(F32))
            first_ref[rows, :] = (normed * gain_ref[...]).astype(BF)
            return carry

        lax.fori_loop(0, 8, chunk, 0)

    for r in range(2):
        rows = slice(r * 512, (r + 1) * 512)
        acc = nn(first_ref[rows, :], w_ref[...])

        @pl.when(j < 4)
        def _():
            scale = jnp.where(j < 2, 0.125, 1.0)
            for i in range(4):
                part = acc[:, i * 128 : (i + 1) * 128]
                turned = part * cos_ref[rows, :] + rotated(part) * sin_ref[rows, :]
                out_ref[rows, i * 128 : (i + 1) * 128] = (turned * scale).astype(BF)

        @pl.when(j >= 4)
        def _():
            out_ref[rows, :] = acc.astype(BF)


def qkv_call(rows_in, gain, w_qkv, cosine, sine):
    whole = lambda shape: pl.BlockSpec(shape, lambda j: (0, 0))
    return pl.pallas_call(
        qkv_kernel,
        grid=(6,),
        out_shape=[jax.ShapeDtypeStruct((1024, 1024), BF), jax.ShapeDtypeStruct((1024, 3072), BF)],
        in_specs=[
            whole((1024, 1024)),
            whole((1, 1024)),
            pl.BlockSpec((1024, 512), lambda j: (0, j)),
            whole((1024, 128)),
            whole((1024, 128)),
        ],
        out_specs=[whole((1024, 1024)), pl.BlockSpec((1024, 512), lambda j: (0, j))],
        cost_estimate=cost(20),
        name="norm_qkv",
    )(rows_in, gain, w_qkv, cosine, sine)


ROWS = 256


def attend_kernel(q_ref, k_ref, v_ref, *refs):
    out_ref, lse_ref = refs[-2:]
    keys, values = k_ref[...], v_ref[...]

    def chunk(i, carry):
        rows = pl.ds(pl.multiple_of(i * ROWS, ROWS), ROWS)
        q = q_ref[rows, :]
        low_half = lax.broadcasted_iota(jnp.int32, (ROWS, 128), 1) < 64
        zero = jnp.zeros_like(q)
        outs, stats = [], []
        for part in (jnp.where(low_half, q, zero), jnp.where(low_half, zero, q)):
            scores = nt(part, keys)
            peak = jnp.max(scores, -1, keepdims=True)
            weights = jnp.exp(scores - peak)
            total = jnp.sum(weights, -1, keepdims=True)
            outs.append(nn(weights.astype(BF), values) / total)
            stats.append(peak + jnp.log(total))
        out_ref[rows, :] = jnp.where(low_half, outs[0], outs[1]).astype(BF)
        lse_ref[rows, :] = jnp.where(low_half, stats[0], stats[1])
        return carry

    lax.fori_loop(0, 1024 // ROWS, chunk, 0)


def head_spec(offset):
    return pl.BlockSpec((1024, 128), lambda j: (0, offset + j))


def attend_call(qkv, start, count, carry):
    operands, in_specs, aliases = [qkv] * 3, [head_spec(i + start) for i in (0, 8, 16)], {}
    if carry is not None:
        operands += list(carry)
        in_specs += [ANY, ANY]
        aliases = {3: 0, 4: 1}
    return pl.pallas_call(
        attend_kernel,
        grid=(count,),
        out_shape=[jax.ShapeDtypeStruct((1024, 1024), BF), jax.ShapeDtypeStruct((1024, 1024), F32)],
        in_specs=in_specs,
        out_specs=[head_spec(start)] * 2,
        input_output_aliases=aliases,
        cost_estimate=cost(5 * count),
        name="attend",
    )(*operands)


def attend_back_kernel(
    q_ref, k_ref, v_ref, att_ref, lse_ref, datt_ref, cos_ref, sin_ref, *refs
):
    out_ref, qt, dt, dkt, dvt = refs[-5:]
    keys, values = k_ref[...], v_ref[...]
    lane = lax.broadcasted_iota(jnp.int32, (1024, 128), 1) < 64
    nothing = jnp.zeros_like(keys)
    key_parts = (jnp.where(lane, keys, nothing), jnp.where(lane, nothing, keys))
    for i in range(1024 // ROWS):
        rows = slice(i * ROWS, (i + 1) * ROWS)
        qt[i] = q_ref[rows, :].astype(F32).T.astype(BF)
        dt[i] = datt_ref[rows, :].astype(F32).T.astype(BF)
    dkt[...] = jnp.zeros_like(dkt)
    dvt[...] = jnp.zeros_like(dvt)

    def chunk(i, carry):
        rows = pl.ds(pl.multiple_of(i * ROWS, ROWS), ROWS)
        q, datt = q_ref[rows, :], datt_ref[rows, :]
        low_half = lax.broadcasted_iota(jnp.int32, (ROWS, 128), 1) < 64
        zero = jnp.zeros_like(q)
        mixed = datt.astype(F32) * att_ref[rows, :].astype(F32)
        grad_q = jnp.zeros((ROWS, 128), F32)
        for h in range(2):
            def pick(t, z):
                return jnp.where(low_half, t, z) if h == 0 else jnp.where(low_half, z, t)

            delta = jnp.sum(pick(mixed, jnp.zeros_like(mixed)), -1, keepdims=True)
            lse = lse_ref[rows, h * 64 : h * 64 + 1]
            probs = jnp.exp(nt(pick(q, zero), keys) - lse)
            grad_probs = nt(pick(datt, zero), values)
            grad_scores = (probs * (grad_probs - delta)).astype(BF)
            grad_q += nn(grad_scores, key_parts[h])
            side = slice(h * 64, (h + 1) * 64)
            dkt[side, :] += nn(qt[i, side, :], grad_scores)
            dvt[side, :] += nn(dt[i, side, :], probs.astype(BF))
        grad_q = grad_q * 0.125
        grad_q = grad_q * cos_ref[rows, :] - rotated(grad_q) * sin_ref[rows, :]
        out_ref[0, rows, :] = grad_q.astype(BF)
        return carry

    lax.fori_loop(0, 1024 // ROWS, chunk, 0)
    grad_k = dkt[...].T
    grad_k = grad_k * cos_ref[...] - rotated(grad_k) * sin_ref[...]
    out_ref[1] = grad_k.astype(BF)
    out_ref[2] = dvt[...].T.astype(BF)


def attend_back_call(qkv, attended, lse, datt, cosine, sine, start, count, carry):
    table = pl.BlockSpec((1024, 128), lambda j: (0, 0))
    operands = [qkv, qkv, qkv, attended, lse, datt, cosine, sine]
    in_specs = [head_spec(i + start) for i in (0, 8, 16, 0, 0, 0)] + [table] * 2
    aliases = {}
    if carry is not None:
        operands.append(carry)
        in_specs.append(ANY)
        aliases = {8: 0}
    return pl.pallas_call(
        attend_back_kernel,
        grid=(count,),
        out_shape=jax.ShapeDtypeStruct((3, 1024, 1024), BF),
        in_specs=in_specs,
        out_specs=pl.BlockSpec((3, 1024, 128), lambda j: (0, 0, start + j)),
        scratch_shapes=[
            pltpu.VMEM((1024 // ROWS, 128, ROWS), BF),
            pltpu.VMEM((1024 // ROWS, 128, ROWS), BF),
            pltpu.VMEM((128, 1024), F32),
            pltpu.VMEM((128, 1024), F32),
        ],
        input_output_aliases=aliases,
        cost_estimate=cost(7.5 * count),
        name="attend_back",
    )(*operands)


def feed_kernel(second_ref, grad_ref, gate_ref, up_ref, down_ref, hid_ref, dgate_ref, dup_ref):
    def chunk(i, carry):
        rows = pl.ds(pl.multiple_of(i * 256, 256), 256)
        second = second_ref[rows, :]
        gate = nn(second, gate_ref[...])
        up = nn(second, up_ref[...])
        grad = nn(grad_ref[rows, :], down_ref[...])
        below = 0.5 + 0.5 * lax.erf(gate * math.sqrt(0.5))
        active = gate * below
        slope = below + gate * jnp.exp(-0.5 * gate * gate) * (1.0 / math.sqrt(2.0 * math.pi))
        hid_ref[rows, :] = (active * up).astype(BF)
        dgate_ref[rows, :] = (grad * up * slope).astype(BF)
        dup_ref[rows, :] = (grad * active).astype(BF)
        return carry

    lax.fori_loop(0, 4, chunk, 0)


def feed_call(second, grad_low, w_gate, w_up, w_down_t):
    width, block = w_gate.shape[1], 896
    rows = pl.BlockSpec((1024, 1024), lambda j: (0, 0))
    cols = pl.BlockSpec((1024, block), lambda j: (0, j))
    return pl.pallas_call(
        feed_kernel,
        grid=(width // block,),
        out_shape=[jax.ShapeDtypeStruct((1024, width), BF)] * 3,
        in_specs=[rows, rows, cols, cols, cols],
        out_specs=[cols] * 3,
        cost_estimate=cost(30),
        name="feed",
    )(second, grad_low, w_gate, w_up, w_down_t)


def whole_rows(local, place):
    own = lax.dynamic_index_in_dim(local, place, 0, keepdims=False)
    got = swap(lax.dynamic_index_in_dim(local, 1 - place, 0, keepdims=False), "x")
    return jnp.where(
        place == 0, jnp.concatenate([own, got], 0), jnp.concatenate([got, own], 0)
    )


def half_rows(whole, place):
    half = whole.shape[0] // 2
    own = lax.dynamic_slice_in_dim(whole, place * half, half, 0)
    got = swap(lax.dynamic_slice_in_dim(whole, (1 - place) * half, half, 0), "x")
    return jnp.where(place == 0, jnp.stack([own, got]), jnp.stack([got, own]))


def paired_body(tokens, cotangent, w_qkv, w_out, w_gate, w_up, w_down, gain_one, gain_two):
    features = w_gate.shape[1]
    padded = -(-features // 896) * 896
    coords = jnp.stack([lax.axis_index(name) for name in BITS]).astype(jnp.int32)
    place = coords[4]
    barrier = lax.optimization_barrier

    def pad(array):
        return jnp.pad(array, ((0, 0), (0, padded - features)))

    gains = jnp.pad(jnp.stack([gain_one, gain_two], 1), ((0, 0), (0, 126)))
    shard_two = jnp.concatenate([pad(w_gate), pad(w_up), w_out], 1)
    shard_three = pad(w_down.T)
    cosine, sine = rotary_tables(1024, 0, HEAD_DIM)
    sign = jnp.where(jnp.arange(HEAD_DIM) < HEAD_DIM // 2, -1.0, 1.0)
    cosine = jnp.concatenate([cosine, cosine], 1)
    sine = jnp.concatenate([sine * sign, sine * sign], 1)

    one = Chain(gather_steps(jnp.concatenate([w_qkv, gains], 1)))
    one.go()
    rows_in = whole_rows(tokens, place)
    one.go()
    shard_two = one.go(shard_two)
    two = Chain(gather_steps(shard_two))
    two.go()
    one.go()
    cotangent, two.waiting = one.go(cotangent, two.waiting)
    grad_low = whole_rows(cotangent, place)
    two.go()
    full_qkv = assemble(one.value, coords, 3072, 1024, 0)
    gain_cols = assemble(one.value, coords, 128, 128, 24)
    full_qkv, shard_three = two.go(full_qkv, shard_three)
    three = Chain(gather_steps(shard_three))
    three.go()
    gain_rows = gain_cols[:, :2].astype(F32).T
    full_one, full_two = gain_rows[0:1], gain_rows[1:2]

    first, qkv = qkv_call(rows_in, full_one, full_qkv, cosine, sine)
    qkv = two.go(qkv)
    qkv = three.go(qkv)
    halves = attend_call(qkv, 0, 3, None)
    halves = three.go(*halves)
    halves = attend_call(qkv, 3, 4, halves)
    halves = three.go(*halves)
    attended, lse = attend_call(qkv, 7, 1, halves)
    attended = two.go(attended)
    full_out = assemble(two.value, coords, 1024, 256, 2 * padded // 256)
    full_gate = assemble(two.value, coords, padded, 896, 0)
    full_up = assemble(two.value, coords, padded, 896, padded // 896)

    inputs_f = rows_in.astype(F32)
    residual = inputs_f + nn(attended, full_out)
    normed_two, inverse_two = standardize(residual)
    second = (normed_two * full_two).astype(BF)
    second, full_gate, full_up = three.go(second, full_gate, full_up)
    full_down = assemble(three.value, coords, padded, 896, 0)
    hidden, d_gate, d_up = feed_call(second, grad_low, full_gate, full_up, full_down)

    block = 896
    col_spec = pl.BlockSpec((1024, block), lambda j: (0, j))
    per = padded // block

    def grad_of(left, right, start, total, carry):
        return grad_call(coords, left, right, col_spec, padded, block, total, start, carry)

    down = Chain(scatter_steps(*grad_of(grad_low, hidden, 0, padded, None)), 2)
    d_gate = down.go(d_gate)
    sums = grad_of(second, d_gate, 0, 2 * padded, None)
    sums, d_up = down.go(sums, d_up)
    sums = grad_of(second, d_up, per, 2 * padded, sums)
    feed = Chain(scatter_steps(*sums), 2)
    d_gate = feed.go(d_gate)
    d_gate = down.go(d_gate)
    grad_second = nt(d_gate, full_gate)
    grad_second, d_up = feed.go(grad_second, d_up)
    grad_second = grad_second + nt(d_up, full_up)
    grad_resid, part_two = norm_back(grad_second, normed_two, inverse_two, full_two)
    grad_resid = grad_resid + grad_low.astype(F32)
    grad_proj = grad_resid.astype(BF)
    grad_proj = down.go(grad_proj)
    datt = nt(grad_proj, full_out).astype(BF)
    out_spec = pl.BlockSpec((1024, 512), lambda j: (0, j))
    out = Chain(
        scatter_steps(*grad_call(coords, attended, grad_proj, out_spec, 1024, 512, 1024, 0, None)),
        2,
    )
    datt = out.go(datt)
    datt = down.go(datt)
    fused = attend_back_call(qkv, attended, lse, datt, cosine, sine, 0, 2, None)
    fused = feed.go(fused)
    fused = out.go(fused)
    fused = attend_back_call(qkv, attended, lse, datt, cosine, sine, 2, 2, fused)
    fused = feed.go(fused)
    fused = out.go(fused)
    outcome = (residual + nt(hidden, full_down)).astype(BF)
    fused, outcome = barrier((fused, outcome))
    result = half_rows(outcome, place)
    fused = attend_back_call(qkv, attended, lse, datt, cosine, sine, 4, 2, fused)
    fused = feed.go(fused)
    fused = out.go(fused)
    fused = attend_back_call(qkv, attended, lse, datt, cosine, sine, 6, 2, fused)
    fused = out.go(fused)

    qkv_spec = pl.BlockSpec((1, 1024, 1024), lambda j: (j, 0, 0))
    last = Chain(
        scatter_steps(*grad_call(coords, first, fused, qkv_spec, 3072, 1024, 3072, 0, None)),
        2,
    )
    fused = last.go(fused)
    grad_first = nt(fused[0], full_qkv[:, :1024])
    grad_first, fused = last.go(grad_first, fused)
    grad_first = grad_first + nt(fused[1], full_qkv[:, 1024:2048])
    grad_first = grad_first + nt(fused[2], full_qkv[:, 2048:])
    grad_first = last.go(grad_first)
    normed_one, inverse_one = standardize(inputs_f)
    grad_in, part_one = norm_back(grad_first, normed_one, inverse_one, full_one)
    input_grad = half_rows((grad_in + grad_resid).astype(BF), place)
    parts = jnp.stack([part_one, part_two])
    for axis in BITS:
        parts = parts + swap(parts, axis)
    index = ((((coords[0] * 2 + coords[1]) * 2 + coords[2]) * 2 + coords[3]) * 2 + coords[4]) * 32
    parts = lax.dynamic_slice_in_dim(parts, index, 32, 1)
    last.go()
    last.go()
    return (
        result,
        input_grad,
        last.value,
        out.value,
        feed.value[:, :features],
        feed.value[:, padded : padded + features],
        down.value[:, :features].T,
        parts[0],
        parts[1],
    )


def solution(mesh):
    groups, pair = mesh.shape["dp"], mesh.shape["ctx"]
    if (groups, pair) == (16, 2):
        mesh = jax.sharding.Mesh(mesh.devices.reshape(2, 2, 2, 2, 2), BITS)
        outer, inner, run = BITS[:4], "x", paired_body
    else:
        outer, inner, run = "dp", "ctx", body
    every = BITS if run is paired_body else ("dp", "ctx")
    whole, rows, cols, line = P(outer, inner, None), P(every, None), P(None, every), P(every)
    in_specs = (whole, whole, rows, rows, rows, rows, cols, line, line)
    out_specs = (whole, whole, rows, rows, rows, rows, cols, line, line)
    return jax.shard_map(run, mesh=mesh, in_specs=in_specs, out_specs=out_specs, check_vma=False)
```
